256 devices in a mesh: dp: 16 (over x, z_hi, core), ctx: 16 (over z_lo, y).
Axes of the slice: x: 4, y: 4, z: 8 (z_hi: 2, z_lo: 4; z = z_hi * 4 + z_lo), core: 2. Of those that a mesh axis runs over, the one named last changes fastest.
Arguments:
- tokens: bfloat16 [16, 4096, 2560], P('dp', 'ctx'), may hold values from -6 to 6
- w_x: bfloat16 [2560, 2560], P(None, 'dp'), may hold values from -0.125 to 0.125
- w_bc: bfloat16 [2560, 256], replicated, may hold values from -0.009765625 to 0.009765625
- w_dt: bfloat16 [2560, 40], replicated, may hold values from -0.125 to 0.125
- dt_bias: float32 [40], replicated, may hold values from -1 to 1
- decay_rate: float32 [40], replicated, may hold values from 0.00012207031 to 0.08
- skip_gain: float32 [40], replicated, may hold values from 0.5 to 1.5
- grad_y: bfloat16 [16, 4096, 2560], P('dp', 'ctx'), may hold values from -6 to 6
Outputs:
- head_out: bfloat16 [16, 4096, 2560], P('dp', 'ctx')
- d_tokens: bfloat16 [16, 4096, 2560], P('dp', 'ctx')
The draws below stay inside these ranges and needn't reach their ends.
All inputs are finite; a program needn't handle non-finite values.
Results may differ from the reference program's by a relative error of at most 0.017.
Values may be sent and summed in bfloat16 or wider, within the bound.
A program may use at most 128 MiB of HBM per device.

```python
import math
import jax
import jax.numpy as jnp
from jax import lax

D = 2560
H = 40
P_SIZE = 64
N = 128
Q = 256
BATCH = 16
LENGTH = 4096
HP = 2560


def block_scale(rng, extent, cuts, smallest, largest):
    level = 1.0
    for axis_at, parts in cuts:
        heights = jax.random.uniform(jax.random.fold_in(jax.random.fold_in(rng, 6), axis_at), (parts,), jnp.float32, smallest / len(cuts), largest / len(cuts))
        level = level * jnp.repeat(jnp.exp(heights), extent[axis_at] // parts).reshape((-1,) + (1,) * (len(extent) - 1 - axis_at))
    return level


def normal_values(rng, shape, scale, reach, cuts=(), dtype=jnp.bfloat16):
    values = scale * jax.random.normal(rng, shape, jnp.float32)
    if cuts:
        values = values * block_scale(rng, shape, cuts, -0.22, 0.18)
    return jnp.clip(values, -reach, reach).astype(dtype)


def setup_inputs(seed: int = 0) -> dict:
    streams_of = jax.random.split(jax.random.key(seed), 9)
    tokens = normal_values(streams_of[0], (BATCH, LENGTH, D), 1.0, 6.0, ((0, 16), (1, 16)))
    w_x = normal_values(streams_of[1], (D, HP), D ** -0.5, 0.125, ((1, 16),))
    w_bc = normal_values(streams_of[2], (D, 2 * N), (D * N) ** -0.5, 0.009765625)
    w_dt = normal_values(streams_of[3], (D, H), D ** -0.5, 0.125)
    dt_bias = jnp.clip(jax.random.uniform(streams_of[4], (H,), jnp.float32, -1.0, 1.0), -1.0, 1.0)
    decay_rate = jnp.clip(jnp.exp(jax.random.uniform(streams_of[5], (H,), jnp.float32, math.log(0.00012207031), math.log(0.08))), 0.00012207031, 0.08)
    skip_gain = jnp.clip(jax.random.uniform(streams_of[6], (H,), jnp.float32, 0.5, 1.5), 0.5, 1.5)
    grad_y = normal_values(streams_of[7], (BATCH, LENGTH, HP), 1.0, 6.0, ((0, 16), (1, 16)))
    return {"tokens": tokens, "w_x": w_x, "w_bc": w_bc, "w_dt": w_dt, "dt_bias": dt_bias, "decay_rate": decay_rate, "skip_gain": skip_gain, "grad_y": grad_y}


HIGHEST_PRECISION = lax.Precision.HIGHEST

def group_rates(raw_block, rate_vec, bias_vec):
    step_size = jax.nn.softplus(raw_block + bias_vec[None, :])
    running = jnp.cumsum(-rate_vec[None, :] * step_size, axis=0)
    return (step_size, running)

def group_forward(entering, pieces, rate_vec, bias_vec, skip_vec):
    x_block, raw_block, b_block, c_block = pieces
    step_size, running = group_rates(raw_block, rate_vec, bias_vec)
    length = x_block.shape[0]
    scores = jnp.dot(c_block, b_block.T, precision=HIGHEST_PRECISION)
    causal = jnp.arange(length)[:, None] >= jnp.arange(length)[None, :]
    by_head = running.T
    spread = by_head[:, :, None] - by_head[:, None, :]
    decays = jnp.exp(jnp.where(causal[None, :, :], spread, -1e+30))
    mixing = scores[None, :, :] * decays * step_size.T[:, None, :]
    within = jnp.einsum('hij,jhp->ihp', mixing, x_block, precision=HIGHEST_PRECISION)
    carried = jnp.einsum('in,hpn->ihp', c_block, entering, precision=HIGHEST_PRECISION) * jnp.exp(running)[:, :, None]
    outputs = within + carried + skip_vec[None, :, None] * x_block
    weights_tail = jnp.exp(running[-1][None, :] - running) * step_size
    updated = jnp.exp(running[-1])[:, None, None] * entering + jnp.einsum('jh,jhp,jn->hpn', weights_tail, x_block, b_block, precision=HIGHEST_PRECISION)
    return (updated, outputs)

def split_blocks(array, count):
    return array.reshape((count, array.shape[0] // count) + array.shape[1:])

def run_block(values, entering, rate_vec, bias_vec, skip_vec):
    x_all = values[0]
    count = x_all.shape[0] // Q

    def advance(carried_in, pieces):
        return group_forward(carried_in, pieces, rate_vec, bias_vec, skip_vec)
    final_state, outputs = lax.scan(advance, entering, tuple((split_blocks(member, count) for member in values)))
    return (outputs.reshape(x_all.shape), final_state)

def reference(tokens, w_x, w_bc, w_dt, dt_bias, decay_rate, skip_gain, grad_y):

    def one_sequence(items):
        tok_rows, grad_rows = items
        x_round = jnp.dot(tok_rows, w_x, preferred_element_type=jnp.float32).astype(jnp.bfloat16)
        bc_round = jnp.dot(tok_rows, w_bc, preferred_element_type=jnp.float32).astype(jnp.bfloat16)
        raw_dt = jnp.dot(tok_rows, w_dt, preferred_element_type=jnp.float32)
        x_float = lax.optimization_barrier(x_round).astype(jnp.float32).reshape(LENGTH, H, P_SIZE)
        bc_float = lax.optimization_barrier(bc_round).astype(jnp.float32)
        b_float = bc_float[:, :N]
        c_float = bc_float[:, N:]
        grad_float = grad_rows.astype(jnp.float32).reshape(LENGTH, H, P_SIZE)
        zero_state = jnp.zeros((H, P_SIZE, N), jnp.float32)

        def forward(x_arg, raw_arg, b_arg, c_arg):
            return run_block((x_arg, raw_arg, b_arg, c_arg), zero_state, decay_rate, dt_bias, skip_gain)[0]
        head_float, backward = jax.vjp(forward, x_float, raw_dt, b_float, c_float)
        grad_x, grad_raw, grad_b, grad_c = backward(grad_float)
        grad_x_round = grad_x.reshape(LENGTH, H * P_SIZE).astype(jnp.bfloat16)
        grad_bc_round = jnp.concatenate([grad_b, grad_c], axis=1).astype(jnp.bfloat16)
        grad_raw_round = grad_raw.astype(jnp.bfloat16)
        contract = (((1,), (1,)), ((), ()))
        total = lax.dot_general(grad_x_round, w_x, contract, preferred_element_type=jnp.float32)
        total = total + lax.dot_general(grad_bc_round, w_bc, contract, preferred_element_type=jnp.float32)
        total = total + lax.dot_general(grad_raw_round, w_dt, contract, preferred_element_type=jnp.float32)
        return (head_float.reshape(LENGTH, H * P_SIZE).astype(jnp.bfloat16), total.astype(jnp.bfloat16))
    head_out, d_tokens = lax.map(one_sequence, (tokens, grad_y))
    return (head_out, d_tokens)
```

```python
import functools

import jax
import jax.numpy as jnp
from jax import lax
from jax.experimental import pallas as pl
from jax.experimental.pallas import tpu as pltpu
from jax.sharding import PartitionSpec as P

MESH = pl.DeviceIdType.MESH
F32 = jnp.float32
BF16 = jnp.bfloat16
HI = lax.Precision.HIGHEST

NN = (((1,), (0,)), ((), ()))
NT = (((1,), (1,)), ((), ()))
TN = (((0,), (0,)), ((), ()))

HEAD = 64
PAIR = 128
PANEL = 160
UNIT = 16
HALF = 80
XUNITS = 15
ZUNITS = 20
STEPS = 28


def mm(a, b, dims=NN):
    return lax.dot_general(a, b, dims, preferred_element_type=F32)


def kernel(
    tok_ref, wt_in, wbc_ref, wdt_ref, par_ref, gy_ref,
    y_ref, dtok_ref,
    wt, x_t, gy_t, xw, gw, gx_t, gx_n, y_t,
    run_s, step_s, sig_s, er_s, tail_s, left_s, a_own, q_s, acc_a, both_s, lam_s,
    bt_s, ct_s, b_s, c_s, st_s, mt_s, dst_s, gbc_s,
    s_loc, g_loc, ent, later, f1, f2, fo, g1, g2, go, tsend, ay, az,
    cp_sem, xs_s, xr_s, zs_s, zr_s, ds_s, dr_s, es_s, er_sem, as_s, ar_s,
):
    dp = lax.axis_index("dp")
    cx = lax.axis_index("ctx")
    x = dp // 4
    zh = (dp // 2) % 2
    c = dp % 2
    zl = cx // 4
    y = cx % 4
    z = zh * 4 + zl
    npair = x_t.shape[0] // PAIR
    own_rows = x_t.shape[0] // 4
    own_heads = own_rows // HEAD
    nhead = run_s.shape[0]

    def at_x(k):
        return (((x + k) % 4) * 4 + zh * 2 + c, cx)

    def at_z(k):
        zz = (z + k + 8) % 8
        return (x * 4 + (zz // 4) * 2 + c, (zz % 4) * 4 + y)

    def at_y(k):
        return (dp, zl * 4 + (y + k) % 4)

    def at_zl(k):
        return (dp, ((zl + k + 4) % 4) * 4 + y)

    sibling = (x * 4 + zh * 2 + (1 - c), cx)

    def remote(src, dst, send, recv, device):
        return pltpu.make_async_remote_copy(
            src_ref=src, dst_ref=dst, send_sem=send, recv_sem=recv,
            device_id=device, device_id_type=MESH,
        )

    def panel_row(xx, half, core):
        return ((xx % 4) * 4 + half * 2 + core) * PANEL

    own = pl.multiple_of(panel_row(x, zh, c), UNIT)
    cp = pltpu.make_async_copy(wt_in, wt.at[pl.ds(own, PANEL)], cp_sem)
    cp.start()

    barrier = pltpu.get_barrier_semaphore()
    peers = [at_x(1), at_x(3), at_z(1), at_z(-1), sibling]
    peers += [at_y(k) for k in (1, 2, 3)] + [at_zl(k) for k in (1, 2, 3)]
    for peer in peers:
        pl.semaphore_signal(barrier, inc=1, device_id=peer, device_id_type=MESH)
    pl.semaphore_wait(barrier, len(peers))
    cp.wait()

    def rows(start, size):
        return wt.at[pl.ds(pl.multiple_of(start, UNIT), size)]

    def x_copy(way, j):
        if way == 0:
            start = jnp.where(
                j < 10, panel_row(x, zh, c) + UNIT * j,
                panel_row(x + 1, zh, c) + UNIT * (j - 10),
            )
            device = at_x(3)
        else:
            start = jnp.where(
                j < 10, panel_row(x, zh, c) + UNIT * ((j + 5) % 10),
                panel_row(x + 3, zh, c) + UNIT * (j - 5),
            )
            device = at_x(1)
        ref = rows(start, UNIT)
        return remote(ref, ref, xs_s.at[way, j], xr_s.at[way, j], device)

    def order(way, g):
        if way == 0:
            return jnp.where(g == 2, 3, jnp.where(g == 3, 2, g))
        return jnp.where(g == 1, 3, jnp.where(g == 2, 1, jnp.where(g == 3, 2, 0)))

    is_source = [zl == 3, zl == 0]

    def z_copy(way, k):
        half = jnp.where(is_source[way], zh, 1 - zh)
        start = panel_row(x + order(way, k // 5), half, c) + UNIT * (k % 5) + HALF * way
        ref = rows(start, UNIT)
        return remote(
            ref, ref, zs_s.at[way, k], zr_s.at[way, k], at_z(1) if way == 0 else at_z(-1)
        )

    def sib_copy(index, start, size):
        ref = rows(start, size)
        return remote(ref, ref, ds_s.at[index], dr_s.at[index], sibling)

    def sib_x(way, t):
        if way == 0:
            start = jnp.where(t == 2, panel_row(x + 2, zh, c), panel_row(x + 1, zh, c) + HALF * (t % 2))
        else:
            start = jnp.where(
                t == 2, panel_row(x + 2, zh, c) + HALF, panel_row(x + 3, zh, c) + HALF * ((t + 1) % 2)
            )
        return sib_copy(2 * t + way, start, HALF)

    def sib_z(way, g):
        start = panel_row(x + order(way, g), 1 - zh, c) + HALF * way
        return sib_copy(6 + 2 * g + way, start, HALF)

    def sib_own():
        ref = rows(own, PANEL)
        return remote(ref, ref, ds_s.at[14], dr_s.at[14], sibling)

    @pl.loop(0, 10)
    def _(j):
        x_copy(0, j).start()
        x_copy(1, j).start()

    for way in (0, 1):
        @pl.when(is_source[way])
        def _():
            @pl.loop(0, 5)
            def _(k):
                z_copy(way, k).start()
    sib_own().start()

    tok = tok_ref[...]
    bc_t = mm(wbc_ref[...], tok, NT)
    nstate = bc_t.shape[0] // 2
    bt_s[...] = bc_t[:nstate].astype(BF16)
    ct_s[...] = bc_t[nstate:].astype(BF16)
    b_s[...] = bc_t[:nstate].T.astype(BF16)
    c_s[...] = bc_t[nstate:].T.astype(BF16)
    raw = mm(wdt_ref[...], tok, NT)[:nhead]
    length = raw.shape[1]
    shifted = raw + par_ref[0]
    step = jnp.maximum(shifted, 0.0) + jnp.log1p(jnp.exp(-jnp.abs(shifted)))
    step_s[...] = step
    sig_s[...] = 1.0 / (1.0 + jnp.exp(-shifted))
    first = lax.broadcasted_iota(jnp.int32, (length, length), 0)
    second = lax.broadcasted_iota(jnp.int32, (length, length), 1)
    upper = jnp.where(first <= second, 1.0, 0.0)
    run = lax.dot_general(-par_ref[1] * step, upper, NN, precision=HI, preferred_element_type=F32)
    run_s[...] = run
    er_s[...] = jnp.exp(run)
    last = run[:, length - 1 :]
    left_s[...] = jnp.exp(last - run)
    tail_s[...] = left_s[...] * step
    a_own[...] = jnp.broadcast_to(jnp.exp(last), a_own.shape)
    st_s[...] = mm(b_s[...], ct_s[...])

    def two(ref, q):
        return jnp.concatenate(
            [jnp.broadcast_to(ref[pl.ds(2 * q + i, 1), :], (HEAD, length)) for i in (0, 1)], axis=0
        )

    def pair_rows(q):
        return pl.ds(pl.multiple_of(q * PAIR, PAIR), PAIR)

    @pl.loop(0, npair)
    def _(q):
        at = pair_rows(q)
        g = gy_ref[:, at].astype(F32).T
        gy_t[at, :] = g.astype(BF16)
        scaled = (g * two(er_s, q)).astype(BF16)
        gw[at, :] = scaled
        g_loc[at, :] = mm(scaled, c_s[...]).astype(BF16)

    def a_y(k):
        return remote(a_own, ay.at[y], as_s.at[k - 1], ar_s.at[k - 1], at_y(k))

    def a_z(k):
        return remote(az.at[zl], az.at[zl], as_s.at[k + 2], ar_s.at[k + 2], at_zl(k))

    for k in (1, 2, 3):
        a_y(k).start()
    ay[y] = a_own[...]

    def my_rows(k):
        return pl.ds(pl.multiple_of(((y + k) % 4) * own_rows, own_rows), own_rows)

    def e_first(src, got, base, k):
        return remote(
            src.at[my_rows(k)], got.at[y], es_s.at[base + k - 1], er_sem.at[base + k - 1], at_y(k)
        )

    def e_total(way, got, base, k):
        device = at_zl(k) if way == 0 else at_zl(-k)
        return remote(
            tsend.at[way], got.at[zl], es_s.at[base + 2 + k], er_sem.at[base + 2 + k], device
        )

    def e_back(out, res, base, k):
        return remote(
            out.at[(y + k) % 4], res.at[my_rows(0)],
            es_s.at[base + 5 + k], er_sem.at[base + 5 + k], at_y(k),
        )

    def begin(src, got, base):
        for k in (1, 2, 3):
            e_first(src, got, base, k).start()
        got[y] = src[my_rows(0), :]

    def head_rows(h):
        return pl.ds(pl.multiple_of(h * HEAD, HEAD), HEAD)

    def decay(ref, slot, h):
        return ref[slot, pl.ds(y * own_heads + h, 1), :]

    def totals(way, src, got1, got2, base):
        for k in (1, 2, 3):
            e_first(src, got1, base, k).wait()
        ys = (0, 1, 2, 3) if way == 0 else (3, 2, 1, 0)

        @pl.loop(0, own_heads)
        def _(h):
            t = got1[ys[0], head_rows(h), :].astype(F32)
            for s in ys[1:]:
                t = decay(ay, s, h) * t + got1[s, head_rows(h), :].astype(F32)
            tsend[way, head_rows(h), :] = t.astype(BF16)

        for k in (1, 2, 3):
            ok = (zl + k < 4) if way == 0 else (zl - k >= 0)

            @pl.when(ok)
            def _():
                e_total(way, got2, base, k).start()

    def spread(way, got1, got2, out, res, base, work):
        for k in (1, 2, 3):
            ok = (zl - k >= 0) if way == 0 else (zl + k < 4)

            @pl.when(ok)
            def _():
                e_total(way, got2, base, k).wait_recv()
        ys = (0, 1, 2, 3) if way == 0 else (3, 2, 1, 0)
        zs = (0, 1, 2) if way == 0 else (3, 2, 1)

        @pl.loop(0, own_heads)
        def _(h):
            work[...] = jnp.zeros_like(work)
            for s in zs:
                @pl.when(s < zl if way == 0 else s > zl)
                def _():
                    work[...] = decay(az, s, h) * work[...] + got2[s, head_rows(h), :].astype(F32)
            e = work[...]
            for s in ys:
                out[s, head_rows(h), :] = e.astype(BF16)
                if s != ys[-1]:
                    e = decay(ay, s, h) * e + got1[s, head_rows(h), :].astype(F32)

        for k in (1, 2, 3):
            e_back(out, res, base, k).start()
        res[my_rows(0), :] = out[y]

    def finish(way, out, res, got2, base):
        for k in (1, 2, 3):
            e_back(out, res, base, k).wait()
            ok = (zl + k < 4) if way == 0 else (zl - k >= 0)

            @pl.when(ok)
            def _():
                e_total(way, got2, base, k).wait_send()

    begin(g_loc, g1, 0)

    for k in (1, 2, 3):
        a_y(k).wait()
    az[zl] = ay[0] * ay[1] * ay[2] * ay[3]
    for k in (1, 2, 3):
        a_z(k).start()

    @pl.loop(0, STEPS)
    def _(s):
        j = s - 2

        @pl.when((j >= 0) & (j < XUNITS))
        def _():
            for way in (0, 1):
                x_copy(way, j).wait_recv()

            @pl.when(j < 5)
            def _():
                for way in (0, 1):
                    x_copy(way, j + 10).start()

            for way in (0, 1):
                @pl.when(is_source[way])
                def _():
                    z_copy(way, j + 5).start()

            @pl.when(j % 5 == 4)
            def _():
                for way in (0, 1):
                    sib_x(way, j // 5).start()

        for way in (0, 1):
            k = s - 2 - 2 * (zl if way == 0 else 3 - zl)

            @pl.when((k >= 0) & (k < ZUNITS))
            def _():
                z_copy(way, k).wait_recv()

                @pl.when(jnp.logical_not(is_source[way]))
                def _():
                    z_copy(way, k).start()

                @pl.when(k % 5 == 4)
                def _():
                    sib_z(way, k // 5).start()

    for k in (1, 2, 3):
        a_z(k).wait()
    totals(1, g_loc, g1, g2, 0)
    spread(1, g1, g2, go, later, 0, lam_s)

    sib_own().wait()
    for t in range(3):
        for way in (0, 1):
            sib_x(way, t).wait()
    for g in range(4):
        for way in (0, 1):
            sib_z(way, g).wait()

    @pl.loop(0, XUNITS)
    def _(j):
        for way in (0, 1):
            x_copy(way, j).wait_send()

    @pl.loop(0, ZUNITS)
    def _(k):
        for way in (0, 1):
            z_copy(way, k).wait_send()

    @pl.loop(0, 4)
    def _(g):
        at = pl.ds(pl.multiple_of(g * own_rows, own_rows), own_rows)
        x_t[at, :] = mm(wt[at, :], tok_ref[...], NT).astype(BF16)

    @pl.loop(0, npair)
    def _(q):
        at = pair_rows(q)
        scaled = (x_t[at, :].astype(F32) * two(tail_s, q)).astype(BF16)
        xw[at, :] = scaled
        s_loc[at, :] = mm(scaled, b_s[...]).astype(BF16)

    begin(s_loc, f1, 9)
    totals(0, s_loc, f1, f2, 9)
    finish(1, go, later, g2, 0)

    dst_s[...] = jnp.zeros_like(dst_s)
    mt_s[...] = jnp.zeros_like(mt_s)
    side = length // 2
    keep = (
        lax.broadcasted_iota(jnp.int32, (side, side), 0)
        <= lax.broadcasted_iota(jnp.int32, (side, side), 1)
    )

    @pl.loop(0, nhead)
    def _(h):
        at = head_rows(h)
        r = run_s[pl.ds(h, 1), :]
        r_col = jnp.broadcast_to(r, (side, length)).T
        e00 = jnp.exp(jnp.where(keep, r[:, :side] - r_col[:side], -1e30))
        e01 = jnp.exp(r[:, side:] - r_col[:side])
        e11 = jnp.exp(jnp.where(keep, r[:, side:] - r_col[side:], -1e30))
        mt_s[:side, :side] = (e00 * st_s[:side, :side]).astype(BF16)
        mt_s[:side, side:] = (e01 * st_s[:side, side:]).astype(BF16)
        mt_s[side:, side:] = (e11 * st_s[side:, side:]).astype(BF16)
        xs = (x_t[at, :].astype(F32) * step_s[pl.ds(h, 1), :]).astype(BF16)
        gy = gy_t[at, :]
        y_t[at, :] = mm(xs, mt_s[...])
        gx_t[at, :] = mm(gy, mt_s[...], NT)
        pull = mm(xs, gy, TN)
        dst_s[:side, :side] += pull[:side, :side] * e00
        dst_s[:side, side:] += pull[:side, side:] * e01
        dst_s[side:, side:] += pull[side:, side:] * e11

    @pl.loop(0, npair)
    def _(q):
        at = pair_rows(q)
        g = gx_t[at, :] + two(left_s, q) * mm(later[at, :], bt_s[...])
        prod = x_t[at, :].astype(F32) * g
        for i in (0, 1):
            q_s[pl.ds(2 * q + i, 1), :] = jnp.sum(
                prod[i * HEAD : (i + 1) * HEAD], axis=0, keepdims=True
            )
        g = g * two(step_s, q) + two(par_ref.at[2], q) * gy_t[at, :].astype(F32)
        gx_n[:, at] = g.T.astype(BF16)

    spread(0, f1, f2, fo, ent, 9, lam_s)
    finish(0, fo, ent, f2, 9)

    @pl.loop(0, npair)
    def _(q):
        at = pair_rows(q)
        inner = y_t[at, :] + two(er_s, q) * mm(ent[at, :], ct_s[...])
        prod = inner * gy_t[at, :].astype(F32)
        full = inner + two(par_ref.at[2], q) * x_t[at, :].astype(F32)
        y_ref[:, at] = full.T.astype(BF16)
        for i in (0, 1):
            acc_a[pl.ds(2 * q + i, 1), :] = jnp.sum(
                prod[i * HEAD : (i + 1) * HEAD], axis=0, keepdims=True
            )
            hr = pl.ds(pl.multiple_of(q * PAIR + i * HEAD, HEAD), HEAD)
            final = a_own[pl.ds(2 * q + i, 1), :] * ent[hr, :].astype(F32) + s_loc[hr, :].astype(F32)
            both = jnp.sum(later[hr, :].astype(F32) * final, axis=0, keepdims=True)
            both_s[pl.ds(2 * q + i, 1), :] = jnp.broadcast_to(
                jnp.sum(both, axis=1, keepdims=True), (1, length)
            )

    dst = dst_s[...].astype(BF16)
    gb_t = mm(ct_s[...], dst, NT) + mm(later[...], xw[...], TN)
    gc_t = mm(bt_s[...], dst) + mm(ent[...], gw[...], TN)
    gbc_s[:, :nstate] = gb_t.T.astype(BF16)
    gbc_s[:, nstate:] = gc_t.T.astype(BF16)
    lower = jnp.where(first >= second, 1.0, 0.0)
    q_all = q_s[...]
    d_log = lax.dot_general(
        acc_a[...] - step_s[...] * q_all, lower, NN, precision=HI, preferred_element_type=F32
    ) + both_s[...]
    g_raw = ((q_all - par_ref[1] * d_log) * sig_s[...]).astype(BF16)

    wide = 512

    @pl.loop(0, dtok_ref.shape[1] // wide)
    def _(n):
        at = pl.ds(pl.multiple_of(n * wide, wide), wide)
        total = mm(gx_n[...], wt[:, at]) + mm(gbc_s[...], wbc_ref[:, at])
        total = total + mm(g_raw, wdt_ref[:nhead, at], TN)
        dtok_ref[:, at] = total.astype(BF16)


def local(tokens, w_x, w_bc, w_dt, dt_bias, decay_rate, skip_gain, grad_y):
    length, width = tokens.shape[1:]
    hp = grad_y.shape[2]
    heads = dt_bias.shape[0]
    state = w_bc.shape[1] // 2
    own = hp // 4
    params = jnp.broadcast_to(
        jnp.stack([dt_bias, decay_rate, skip_gain])[:, :, None], (3, heads, length)
    )
    vmem = pl.BlockSpec(memory_space=pltpu.VMEM)
    flat = pltpu.VMEM((hp, length), BF16)
    wide = pltpu.VMEM((hp, length), F32)
    per_head = pltpu.VMEM((heads, length), F32)
    states = pltpu.VMEM((hp, state), BF16)
    slots = pltpu.VMEM((4, own, state), BF16)
    decays = pltpu.VMEM((heads, state), F32)
    dma = pltpu.SemaphoreType.DMA
    y, dtok = pl.pallas_call(
        kernel,
        out_shape=(
            jax.ShapeDtypeStruct((length, hp), BF16),
            jax.ShapeDtypeStruct((length, width), BF16),
        ),
        in_specs=[vmem] * 6,
        out_specs=(vmem, vmem),
        scratch_shapes=[
            pltpu.VMEM((hp, width), BF16), flat, flat, flat, flat, wide,
            pltpu.VMEM((length, hp), BF16), wide,
            per_head, per_head, per_head, per_head, per_head, per_head, decays,
            per_head, per_head, per_head,
            pltpu.VMEM((HEAD, state), F32),
            pltpu.VMEM((state, length), BF16), pltpu.VMEM((state, length), BF16),
            pltpu.VMEM((length, state), BF16), pltpu.VMEM((length, state), BF16),
            pltpu.VMEM((length, length), F32), pltpu.VMEM((length, length), BF16),
            pltpu.VMEM((length, length), F32), pltpu.VMEM((length, 2 * state), BF16),
            states, states, states, states, slots, slots, slots, slots, slots, slots,
            pltpu.VMEM((2, own, state), BF16),
            pltpu.VMEM((4, heads, state), F32), pltpu.VMEM((4, heads, state), F32),
            dma, dma((2, XUNITS)), dma((2, XUNITS)), dma((2, ZUNITS)), dma((2, ZUNITS)),
            dma((15,)), dma((15,)), dma((18,)), dma((18,)), dma((6,)), dma((6,)),
        ],
        compiler_params=pltpu.CompilerParams(
            collective_id=0, has_side_effects=True, vmem_limit_bytes=60 << 20
        ),
    )(tokens[0], w_x.T, w_bc.T, w_dt.T, params, grad_y[0])
    return (y[None], dtok[None])


def solution(mesh):
    placed = (P("dp", "ctx", None), P(None, "dp"), P(), P(), P(), P(), P(), P("dp", "ctx", None))
    return jax.shard_map(
        local,
        mesh=mesh,
        in_specs=placed,
        out_specs=(P("dp", "ctx", None), P("dp", "ctx", None)),
        check_vma=False,
    )
```

```python
import functools

import jax
import jax.numpy as jnp
from jax import lax
from jax.experimental import pallas as pl
from jax.experimental.pallas import tpu as pltpu
from jax.sharding import PartitionSpec as P

MESH = pl.DeviceIdType.MESH
F32 = jnp.float32
BF16 = jnp.bfloat16
HI = lax.Precision.HIGHEST

NN = (((1,), (0,)), ((), ()))
NT = (((1,), (1,)), ((), ()))
TN = (((0,), (0,)), ((), ()))

HEAD = 64
PAIR = 128
PANEL = 160
UNIT = 16
HALF = 80
XUNITS = 15
ZUNITS = 20
STEPS = 41
GATHER = 28
ENTER = (12, 22, 23, 28)
LEAVE = (24, 35, 36, 40)
BLOCK = 32
DTOK_FROM = 30


def mm(a, b, dims=NN):
    return lax.dot_general(a, b, dims, preferred_element_type=F32)


def kernel(
    tok_ref, wt_in, wbc_ref, wdt_ref, par_ref, gy_ref,
    y_ref, dtok_ref,
    wt, x_t, gy_t, xw, gw, gx_t, gx_n, y_t, acc_d, e_all, m_all,
    run_s, step_s, sig_s, er_s, tail_s, left_s, a_own, q_s, acc_a, both_s,
    bt_s, ct_s, b_s, c_s, st_s, dst_s, gbc_s,
    s_loc, g_loc, ent, later, first_f, total_f, enter_f, pass_f, out_f,
    first_b, total_b, enter_b, pass_b, out_b, ay,
    cp_sem, xs_s, xr_s, zs_s, zr_s, ds_s, dr_s, es_s, er_sem, as_s, ar_s,
):
    dp = lax.axis_index("dp")
    cx = lax.axis_index("ctx")
    x = dp // 4
    zh = (dp // 2) % 2
    c = dp % 2
    zl = cx // 4
    y = cx % 4
    z = zh * 4 + zl
    group = x_t.shape[0] // 4
    group_heads = group // HEAD
    group_pairs = group // PAIR
    slice_rows = group // 4
    nhead = run_s.shape[0]

    def at_x(k):
        return (((x + k) % 4) * 4 + zh * 2 + c, cx)

    def at_z(k):
        zz = (z + k + 8) % 8
        return (x * 4 + (zz // 4) * 2 + c, (zz % 4) * 4 + y)

    def at_y(k):
        return (dp, zl * 4 + (y + k) % 4)

    sibling = (x * 4 + zh * 2 + (1 - c), cx)

    def remote(src, dst, send, recv, device):
        return pltpu.make_async_remote_copy(
            src_ref=src, dst_ref=dst, send_sem=send, recv_sem=recv,
            device_id=device, device_id_type=MESH,
        )

    def panel_row(xx, half, core):
        return ((xx % 4) * 4 + half * 2 + core) * PANEL

    own = pl.multiple_of(panel_row(x, zh, c), UNIT)
    cp = pltpu.make_async_copy(wt_in, wt.at[pl.ds(own, PANEL)], cp_sem)
    cp.start()

    barrier = pltpu.get_barrier_semaphore()
    peers = [at_x(1), at_x(3), at_z(1), at_z(-1), sibling]
    peers += [at_y(k) for k in (1, 2, 3)]
    for peer in peers:
        pl.semaphore_signal(barrier, inc=1, device_id=peer, device_id_type=MESH)
    pl.semaphore_wait(barrier, len(peers))
    cp.wait()

    def rows(start, size):
        return wt.at[pl.ds(pl.multiple_of(start, UNIT), size)]

    def x_copy(way, j):
        if way == 0:
            start = jnp.where(
                j < 10, panel_row(x, zh, c) + UNIT * j,
                panel_row(x + 1, zh, c) + UNIT * (j - 10),
            )
            device = at_x(3)
        else:
            start = jnp.where(
                j < 10, panel_row(x, zh, c) + UNIT * ((j + 5) % 10),
                panel_row(x + 3, zh, c) + UNIT * (j - 5),
            )
            device = at_x(1)
        ref = rows(start, UNIT)
        return remote(ref, ref, xs_s.at[way, j], xr_s.at[way, j], device)

    def order(way, g):
        if way == 0:
            return jnp.where(g == 2, 3, jnp.where(g == 3, 2, g))
        return jnp.where(g == 1, 3, jnp.where(g == 2, 1, jnp.where(g == 3, 2, 0)))

    is_source = [zl == 3, zl == 0]

    def z_copy(way, k):
        half = jnp.where(is_source[way], zh, 1 - zh)
        start = panel_row(x + order(way, k // 5), half, c) + UNIT * (k % 5) + HALF * way
        ref = rows(start, UNIT)
        return remote(
            ref, ref, zs_s.at[way, k], zr_s.at[way, k], at_z(1) if way == 0 else at_z(-1)
        )

    def sib_copy(index, start, size):
        ref = rows(start, size)
        return remote(ref, ref, ds_s.at[index], dr_s.at[index], sibling)

    def sib_x(way, t):
        if way == 0:
            start = jnp.where(t == 2, panel_row(x + 2, zh, c), panel_row(x + 1, zh, c) + HALF * (t % 2))
        else:
            start = jnp.where(
                t == 2, panel_row(x + 2, zh, c) + HALF, panel_row(x + 3, zh, c) + HALF * ((t + 1) % 2)
            )
        return sib_copy(2 * t + way, start, HALF)

    def sib_z(way, g):
        start = panel_row(x + order(way, g), 1 - zh, c) + HALF * way
        return sib_copy(6 + 2 * g + way, start, HALF)

    def sib_own():
        ref = rows(own, PANEL)
        return remote(ref, ref, ds_s.at[14], dr_s.at[14], sibling)

    @pl.loop(0, 10)
    def _(j):
        x_copy(0, j).start()
        x_copy(1, j).start()

    for way in (0, 1):
        @pl.when(is_source[way])
        def _():
            @pl.loop(0, 5)
            def _(k):
                z_copy(way, k).start()
    sib_own().start()

    tok = tok_ref[...]
    bc_t = mm(wbc_ref[...], tok, NT)
    nstate = bc_t.shape[0] // 2
    bt_s[...] = bc_t[:nstate].astype(BF16)
    ct_s[...] = bc_t[nstate:].astype(BF16)
    b_s[...] = bc_t[:nstate].T.astype(BF16)
    c_s[...] = bc_t[nstate:].T.astype(BF16)
    raw = mm(wdt_ref[...], tok, NT)[:nhead]
    length = raw.shape[1]
    shifted = raw + par_ref[0]
    step = jnp.maximum(shifted, 0.0) + jnp.log1p(jnp.exp(-jnp.abs(shifted)))
    step_s[...] = step
    sig_s[...] = 1.0 / (1.0 + jnp.exp(-shifted))
    first = lax.broadcasted_iota(jnp.int32, (length, length), 0)
    second = lax.broadcasted_iota(jnp.int32, (length, length), 1)
    upper = jnp.where(first <= second, 1.0, 0.0)
    run = lax.dot_general(-par_ref[1] * step, upper, NN, precision=HI, preferred_element_type=F32)
    run_s[...] = run
    er_s[...] = jnp.exp(run)
    last = run[:, length - 1 :]
    left_s[...] = jnp.exp(last - run)
    tail_s[...] = left_s[...] * step
    a_own[...] = jnp.broadcast_to(jnp.exp(last), a_own.shape)
    st_s[...] = mm(b_s[...], ct_s[...])

    def two(ref, q):
        return jnp.concatenate(
            [jnp.broadcast_to(ref[pl.ds(2 * q + i, 1), :], (HEAD, length)) for i in (0, 1)], axis=0
        )

    def pair_rows(q):
        return pl.ds(pl.multiple_of(q * PAIR, PAIR), PAIR)

    def a_y(k):
        return remote(a_own, ay.at[y], as_s.at[k - 1], ar_s.at[k - 1], at_y(k))

    for k in (1, 2, 3):
        a_y(k).start()
    ay[y] = a_own[...]

    def head_rows(h):
        return pl.ds(pl.multiple_of(h * HEAD, HEAD), HEAD)

    def group_base(way, g):
        return ((x + order(0, g)) % 4 if way == 0 else g) * group

    src_of = (s_loc, g_loc)
    first_of = (first_f, first_b)
    total_of = (total_f, total_b)
    enter_of = (enter_f, enter_b)
    pass_of = (pass_f, pass_b)
    out_of = (out_f, out_b)
    res_of = (ent, later)
    ys_of = ((0, 1, 2, 3), (3, 2, 1, 0))
    starts = (zl == 0, zl == 3)
    ends = (zl == 3, zl == 0)

    def slice_at(way, g, k):
        start = group_base(way, g) + ((y + k) % 4) * slice_rows
        return pl.ds(pl.multiple_of(start, UNIT), slice_rows)

    def e_first(way, g, k):
        return remote(
            src_of[way].at[slice_at(way, g, k)], first_of[way].at[g, y],
            es_s.at[way, g, k - 1], er_sem.at[way, g, k - 1], at_y(k),
        )

    def e_pass(way, g):
        return remote(
            pass_of[way].at[g], enter_of[way].at[g], es_s.at[way, g, 3], er_sem.at[way, g, 3],
            at_z(1) if way == 0 else at_z(-1),
        )

    def e_back(way, g, k):
        return remote(
            out_of[way].at[g, (y + k) % 4], res_of[way].at[slice_at(way, g, 0)],
            es_s.at[way, g, 3 + k], er_sem.at[way, g, 3 + k], at_y(k),
        )

    def begin(way, g):
        for k in (1, 2, 3):
            e_first(way, g, k).start()
        first_of[way][g, y] = src_of[way][slice_at(way, g, 0), :]

    def block_rows(b):
        return pl.ds(pl.multiple_of(b * BLOCK, BLOCK), BLOCK)

    def block_decay(way, g, b):
        h = group_base(way, g) // HEAD + (y * slice_rows + b * BLOCK) // HEAD
        return [ay[s, pl.ds(h, 1), :] for s in range(4)]

    def totals(way, g):
        for k in (1, 2, 3):
            e_first(way, g, k).wait_recv()

        @pl.loop(0, slice_rows // BLOCK)
        def _(b):
            at = block_rows(b)
            d = block_decay(way, g, b)
            ys = ys_of[way]
            t = first_of[way][g, ys[0], at, :].astype(F32)
            for s in ys[1:]:
                t = d[s] * t + first_of[way][g, s, at, :].astype(F32)
            total_of[way][g, at, :] = t
            pass_of[way][g, at, :] = t.astype(BF16)

        @pl.when(starts[way])
        def _():
            e_pass(way, g).start()
            enter_of[way][g] = jnp.zeros(enter_of[way].shape[1:], BF16)

    def chain(way, g):
        @pl.when(jnp.logical_not(starts[way]))
        def _():
            e_pass(way, g).wait_recv()

            @pl.when(jnp.logical_not(ends[way]))
            def _():
                @pl.loop(0, slice_rows // BLOCK)
                def _(b):
                    at = block_rows(b)
                    d = block_decay(way, g, b)
                    e = enter_of[way][g, at, :].astype(F32)
                    e = d[0] * d[1] * d[2] * d[3] * e + total_of[way][g, at, :]
                    pass_of[way][g, at, :] = e.astype(BF16)

                e_pass(way, g).start()

        @pl.loop(0, slice_rows // BLOCK)
        def _(b):
            at = block_rows(b)
            d = block_decay(way, g, b)
            ys = ys_of[way]
            e = enter_of[way][g, at, :].astype(F32)
            for s in ys:
                out_of[way][g, s, at, :] = e.astype(BF16)
                if s != ys[-1]:
                    e = d[s] * e + first_of[way][g, s, at, :].astype(F32)

        for k in (1, 2, 3):
            e_back(way, g, k).start()
        res_of[way][slice_at(way, g, 0), :] = out_of[way][g, y]

    def finish(way, g):
        for k in (1, 2, 3):
            e_back(way, g, k).wait_recv()

    def drain(way, g):
        for k in (1, 2, 3):
            e_first(way, g, k).wait_send()
            e_back(way, g, k).wait_send()

        @pl.when(jnp.logical_not(ends[way]))
        def _():
            e_pass(way, g).wait_send()

    side = length // 2
    keep = (
        lax.broadcasted_iota(jnp.int32, (side, side), 0)
        <= lax.broadcasted_iota(jnp.int32, (side, side), 1)
    )
    dst_s[...] = jnp.zeros_like(dst_s)

    def own_states(q):
        at = pair_rows(q)
        g = gy_ref[:, at].astype(F32).T
        gy_t[at, :] = g.astype(BF16)
        scaled = (g * two(er_s, q)).astype(BF16)
        gw[at, :] = scaled
        g_loc[at, :] = mm(scaled, c_s[...]).astype(BF16)

    def mixing(h):
        at = head_rows(h)
        r = run_s[pl.ds(h, 1), :]
        r_col = jnp.broadcast_to(r, (side, length)).T
        e00 = jnp.exp(jnp.where(keep, r[:, :side] - r_col[:side], -1e30))
        e01 = jnp.exp(r[:, side:] - r_col[:side])
        e11 = jnp.exp(jnp.where(keep, r[:, side:] - r_col[side:], -1e30))
        e_all[h, :side, :side] = e00.astype(BF16)
        e_all[h, :side, side:] = e01.astype(BF16)
        e_all[h, side:, side:] = e11.astype(BF16)
        m_all[h, :side, :side] = (e00 * st_s[:side, :side]).astype(BF16)
        m_all[h, :side, side:] = (e01 * st_s[:side, side:]).astype(BF16)
        m_all[h, side:, :side] = jnp.zeros((side, side), BF16)
        m_all[h, side:, side:] = (e11 * st_s[side:, side:]).astype(BF16)
        gx_t[at, :] = mm(gy_t[at, :], m_all[h], NT)

    def pull_back(q):
        at = pair_rows(q)
        g = gx_t[at, :] + two(left_s, q) * mm(later[at, :], bt_s[...])
        gx_t[at, :] = g
        g = g * two(step_s, q) + two(par_ref.at[2], q) * gy_t[at, :].astype(F32)
        gx_n[:, at] = g.T.astype(BF16)

    def project(g):
        base = group_base(0, g)
        at = pl.ds(pl.multiple_of(base, group), group)
        x_t[at, :] = mm(wt[at, :], tok_ref[...], NT).astype(BF16)

        @pl.loop(0, group_pairs)
        def _(i):
            q = base // PAIR + i
            here = pair_rows(q)
            scaled = (x_t[here, :].astype(F32) * two(tail_s, q)).astype(BF16)
            xw[here, :] = scaled
            s_loc[here, :] = mm(scaled, b_s[...]).astype(BF16)

    def inside(h):
        at = head_rows(h)
        xh = x_t[at, :].astype(F32)
        xs = (xh * step_s[pl.ds(h, 1), :]).astype(BF16)
        gy = gy_t[at, :]
        y_t[at, :] = mm(xs, m_all[h])
        pull = mm(xs, gy, TN)
        dst_s[:side, :side] += pull[:side, :side] * e_all[h, :side, :side].astype(F32)
        dst_s[:side, side:] += pull[:side, side:] * e_all[h, :side, side:].astype(F32)
        dst_s[side:, side:] += pull[side:, side:] * e_all[h, side:, side:].astype(F32)

    def outputs(q):
        at = pair_rows(q)
        xq = x_t[at, :].astype(F32)
        inner = y_t[at, :] + two(er_s, q) * mm(ent[at, :], ct_s[...])
        prod = inner * gy_t[at, :].astype(F32)
        back = xq * gx_t[at, :]
        full = inner + two(par_ref.at[2], q) * xq
        y_ref[:, at] = full.T.astype(BF16)
        for i in (0, 1):
            part = slice(i * HEAD, (i + 1) * HEAD)
            acc_a[pl.ds(2 * q + i, 1), :] = jnp.sum(prod[part], axis=0, keepdims=True)
            q_s[pl.ds(2 * q + i, 1), :] = jnp.sum(back[part], axis=0, keepdims=True)
            hr = head_rows(2 * q + i)
            final = a_own[pl.ds(2 * q + i, 1), :] * ent[hr, :].astype(F32) + s_loc[hr, :].astype(F32)
            both = jnp.sum(later[hr, :].astype(F32) * final, axis=0, keepdims=True)
            both_s[pl.ds(2 * q + i, 1), :] = jnp.broadcast_to(
                jnp.sum(both, axis=1, keepdims=True), (1, length)
            )

    wide = dtok_ref.shape[1] // 5

    def columns(n):
        return pl.ds(pl.multiple_of(n * wide, 128), wide)

    def pick(s, table):
        found = -1
        for i, t in enumerate(table):
            found = jnp.where(s == t, i, found)
        return found

    @pl.loop(0, STEPS)
    def _(s):
        j = s - 2

        @pl.when((j >= 0) & (j < XUNITS))
        def _():
            for way in (0, 1):
                x_copy(way, j).wait_recv()

            @pl.when(j < 5)
            def _():
                for way in (0, 1):
                    x_copy(way, j + 10).start()

            for way in (0, 1):
                @pl.when(is_source[way])
                def _():
                    z_copy(way, j + 5).start()

            @pl.when(j % 5 == 4)
            def _():
                for way in (0, 1):
                    sib_x(way, j // 5).start()

        for way in (0, 1):
            k = s - 2 - 2 * (zl if way == 0 else 3 - zl)

            @pl.when((k >= 0) & (k < ZUNITS))
            def _():
                z_copy(way, k).wait_recv()

                @pl.when(jnp.logical_not(is_source[way]))
                def _():
                    z_copy(way, k).start()

                @pl.when(k % 5 == 4)
                def _():
                    sib_z(way, k // 5).start()

        @pl.when(s == 2)
        def _():
            for k in (1, 2, 3):
                a_y(k).wait()

        b = s - 3

        @pl.when((b >= 0) & (b < 4))
        def _():
            totals(1, b)

        b = s - 4 - 2 * (3 - zl)

        @pl.when((b >= 0) & (b < 4))
        def _():
            chain(1, b)

        g_total = pick(s - 2, ENTER)

        @pl.when(g_total >= 0)
        def _():
            totals(0, g_total)

        g_chain = pick(s - 3 - 2 * zl, ENTER)

        @pl.when(g_chain >= 0)
        def _():
            chain(0, g_chain)

        g_enter = pick(s, ENTER)

        @pl.when(g_enter >= 0)
        def _():
            @pl.when(g_enter == 0)
            def _():
                sib_own().wait_recv()

            @pl.when(g_enter > 0)
            def _():
                sib_copy(jnp.where(g_enter == 3, 4, g_enter - 1), 0, HALF).wait_recv()
                sib_copy(jnp.where(g_enter == 3, 5, g_enter + 1), 0, HALF).wait_recv()

            swapped = jnp.where(g_enter == 1, 2, jnp.where(g_enter == 2, 1, g_enter))
            sib_copy(6 + 2 * g_enter, 0, HALF).wait_recv()
            sib_copy(7 + 2 * swapped, 0, HALF).wait_recv()
            project(g_enter)
            begin(0, g_enter)

        @pl.when(s < 4)
        def _():
            @pl.loop(0, group_pairs)
            def _(i):
                own_states(s * group_pairs + i)

            begin(1, s)

        @pl.when((s >= 4) & (s < 14))
        def _():
            @pl.loop(0, 4)
            def _(i):
                mixing((s - 4) * 4 + i)

        b = s - 13

        @pl.when((b >= 0) & (b < 4))
        def _():
            finish(1, b)

            @pl.loop(0, group_pairs)
            def _(i):
                pull_back(b * group_pairs + i)

        def inside_some(first_step, g0, count):
            per = group_heads * count // 5
            n = s - first_step

            @pl.when((n >= 0) & (n < 5))
            def _():
                @pl.loop(0, per)
                def _(i):
                    e = n * per + i
                    g = g0 + e // group_heads
                    inside(group_base(0, g) // HEAD + e % group_heads)

        inside_some(17, 0, 1)
        inside_some(24, 1, 2)
        inside_some(29, 3, 1)

        n = s - DTOK_FROM

        @pl.when((n >= 0) & (n < 5))
        def _():
            acc_d[:, columns(n)] = mm(gx_n[...], wt[:, columns(n)])

        g_leave = pick(s, LEAVE)

        @pl.when(g_leave >= 0)
        def _():
            finish(0, g_leave)

            @pl.loop(0, group_pairs)
            def _(i):
                outputs(group_base(0, g_leave) // PAIR + i)

    dst = dst_s[...].astype(BF16)
    gb_t = mm(ct_s[...], dst, NT) + mm(later[...], xw[...], TN)
    gc_t = mm(bt_s[...], dst) + mm(ent[...], gw[...], TN)
    gbc_s[:, :nstate] = gb_t.T.astype(BF16)
    gbc_s[:, nstate:] = gc_t.T.astype(BF16)
    lower = jnp.where(first >= second, 1.0, 0.0)
    q_all = q_s[...]
    d_log = lax.dot_general(
        acc_a[...] - step_s[...] * q_all, lower, NN, precision=HI, preferred_element_type=F32
    ) + both_s[...]
    g_raw = ((q_all - par_ref[1] * d_log) * sig_s[...]).astype(BF16)

    @pl.loop(0, 5)
    def _(n):
        at = columns(n)
        total = acc_d[:, at] + mm(gbc_s[...], wbc_ref[:, at])
        total = total + mm(g_raw, wdt_ref[:nhead, at], TN)
        dtok_ref[:, at] = total.astype(BF16)

    sib_own().wait_send()
    for t in range(3):
        for way in (0, 1):
            sib_x(way, t).wait_send()
    for g in range(4):
        for way in (0, 1):
            sib_z(way, g).wait_send()

    @pl.loop(0, XUNITS)
    def _(j):
        for way in (0, 1):
            x_copy(way, j).wait_send()

    @pl.loop(0, ZUNITS)
    def _(k):
        for way in (0, 1):
            z_copy(way, k).wait_send()

    @pl.loop(0, 4)
    def _(g):
        for way in (0, 1):
            drain(way, g)


def local(tokens, w_x, w_bc, w_dt, dt_bias, decay_rate, skip_gain, grad_y):
    length, width = tokens.shape[1:]
    hp = grad_y.shape[2]
    heads = dt_bias.shape[0]
    state = w_bc.shape[1] // 2
    piece = hp // 16
    params = jnp.broadcast_to(
        jnp.stack([dt_bias, decay_rate, skip_gain])[:, :, None], (3, heads, length)
    )
    vmem = pl.BlockSpec(memory_space=pltpu.VMEM)
    flat = pltpu.VMEM((hp, length), BF16)
    wide = pltpu.VMEM((hp, length), F32)
    per_head = pltpu.VMEM((heads, length), F32)
    states = pltpu.VMEM((hp, state), BF16)
    slots = pltpu.VMEM((4, 4, piece, state), BF16)
    single = pltpu.VMEM((4, piece, state), BF16)
    exact = pltpu.VMEM((4, piece, state), F32)
    exchange = [slots, exact, single, single, slots]
    decays = pltpu.VMEM((heads, state), F32)
    dma = pltpu.SemaphoreType.DMA
    y, dtok = pl.pallas_call(
        kernel,
        out_shape=(
            jax.ShapeDtypeStruct((length, hp), BF16),
            jax.ShapeDtypeStruct((length, width), BF16),
        ),
        in_specs=[vmem] * 6,
        out_specs=(vmem, vmem),
        scratch_shapes=[
            pltpu.VMEM((hp, width), BF16), flat, flat, flat, flat, wide,
            pltpu.VMEM((length, hp), BF16), wide, pltpu.VMEM((length, width), F32),
            pltpu.VMEM((heads, length, length), BF16), pltpu.VMEM((heads, length, length), BF16),
            per_head, per_head, per_head, per_head, per_head, per_head, decays,
            per_head, per_head, per_head,
            pltpu.VMEM((state, length), BF16), pltpu.VMEM((state, length), BF16),
            pltpu.VMEM((length, state), BF16), pltpu.VMEM((length, state), BF16),
            pltpu.VMEM((length, length), F32), pltpu.VMEM((length, length), F32),
            pltpu.VMEM((length, 2 * state), BF16),
            states, states, states, states, *exchange, *exchange,
            pltpu.VMEM((4, heads, state), F32),
            dma, dma((2, XUNITS)), dma((2, XUNITS)), dma((2, ZUNITS)), dma((2, ZUNITS)),
            dma((15,)), dma((15,)), dma((2, 4, 7)), dma((2, 4, 7)), dma((3,)), dma((3,)),
        ],
        compiler_params=pltpu.CompilerParams(
            collective_id=0, has_side_effects=True, vmem_limit_bytes=60 << 20
        ),
    )(tokens[0], w_x.T, w_bc.T, w_dt.T, params, grad_y[0])
    return (y[None], dtok[None])


def solution(mesh):
    placed = (P("dp", "ctx", None), P(None, "dp"), P(), P(), P(), P(), P(), P("dp", "ctx", None))
    return jax.shard_map(
        local,
        mesh=mesh,
        in_specs=placed,
        out_specs=(P("dp", "ctx", None), P("dp", "ctx", None)),
        check_vma=False,
    )
```

```python
import functools

import jax
import jax.numpy as jnp
from jax import lax
from jax.experimental import pallas as pl
from jax.experimental.pallas import tpu as pltpu
from jax.sharding import PartitionSpec as P

MESH = pl.DeviceIdType.MESH
F32 = jnp.float32
BF16 = jnp.bfloat16
HI = lax.Precision.HIGHEST

NN = (((1,), (0,)), ((), ()))
NT = (((1,), (1,)), ((), ()))
TN = (((0,), (0,)), ((), ()))

HEAD = 64
PAIR = 128
PANEL = 160
UNIT = 16
HALF = 80
XUNITS = 18
XOWN = 15
ZUNITS = 17
LAG = 2
STEPS = 33
ENTER = (12, 22, 23, 25)
LEAVE = (24, 28, 30, 32)
INSIDE = ((17, 0, 1), (24, 1, 2), (26, 3, 1))
PUSHED = (1, 2, 3)
BLOCK = 32
DTOK_FROM = 27


def mm(a, b, dims=NN):
    return lax.dot_general(a, b, dims, preferred_element_type=F32)


def kernel(
    tok_in, wt_in, wbc_in, wdt_ref, par_ref, gy_in,
    y_ref, dtok_ref,
    tok_ref, wbc_ref, gy_ref, wt, x_t, gy_t, xw, gw, gx_t, gx_n, y_t, acc_d, e_all, m_all,
    run_s, step_s, sig_s, er_s, tail_s, left_s, a_own, q_s, acc_a, both_s,
    bt_s, ct_s, b_s, c_s, st_s, dst_s, gbc_s,
    s_loc, g_loc, ent, later, first_f, total_f, enter_f, pass_f, out_f,
    first_b, total_b, enter_b, pass_b, out_b, ay,
    az, push_f,
    cp_sem, xs_s, xr_s, zs_s, zr_s, ds_s, dr_s, es_s, er_sem, as_s, ar_s, ps_s, pr_s,
):
    dp = lax.axis_index("dp")
    cx = lax.axis_index("ctx")
    x = dp // 4
    zh = (dp // 2) % 2
    c = dp % 2
    zl = cx // 4
    y = cx % 4
    z = zh * 4 + zl
    group = x_t.shape[0] // 4
    group_heads = group // HEAD
    group_pairs = group // PAIR
    slice_rows = group // 4
    nhead = run_s.shape[0]

    def at_x(k):
        return (((x + k) % 4) * 4 + zh * 2 + c, cx)

    def at_z(k):
        zz = (z + k + 8) % 8
        return (x * 4 + (zz // 4) * 2 + c, (zz % 4) * 4 + y)

    def at_y(k):
        return (dp, zl * 4 + (y + k) % 4)

    def at_zl(k):
        return (dp, ((zl + k + 4) % 4) * 4 + y)

    sibling = (x * 4 + zh * 2 + (1 - c), cx)

    def remote(src, dst, send, recv, device):
        return pltpu.make_async_remote_copy(
            src_ref=src, dst_ref=dst, send_sem=send, recv_sem=recv,
            device_id=device, device_id_type=MESH,
        )

    def panel_row(xx, half, core):
        return ((xx % 4) * 4 + half * 2 + core) * PANEL

    own = pl.multiple_of(panel_row(x, zh, c), UNIT)
    cp = pltpu.make_async_copy(wt_in, wt.at[pl.ds(own, PANEL)], cp_sem.at[0])
    loads = [
        pltpu.make_async_copy(src, dst, cp_sem.at[i + 1])
        for i, (src, dst) in enumerate(((tok_in, tok_ref), (wbc_in, wbc_ref), (gy_in, gy_ref)))
    ]
    cp.start()
    for load in loads:
        load.start()

    barrier = pltpu.get_barrier_semaphore()
    peers = [at_x(1), at_x(3), at_z(1), at_z(-1), sibling]
    peers += [at_y(k) for k in (1, 2, 3)] + [at_zl(k) for k in (1, 2, 3)]
    for peer in peers:
        pl.semaphore_signal(barrier, inc=1, device_id=peer, device_id_type=MESH)
    pl.semaphore_wait(barrier, len(peers))
    cp.wait()

    def rows(start, size):
        return wt.at[pl.ds(pl.multiple_of(start, UNIT), size)]

    def x_copy(way, j):
        if way == 0:
            start = jnp.where(
                j < 10, panel_row(x, zh, c) + UNIT * j,
                jnp.where(
                    j < XOWN, panel_row(x + 1, zh, c) + UNIT * (j - 10),
                    panel_row(x + 1, 1 - zh, c) + UNIT * (j - 13),
                ),
            )
            device = at_x(3)
        else:
            start = jnp.where(
                j < 10, panel_row(x, zh, c) + UNIT * ((j + 5) % 10),
                jnp.where(
                    j < XOWN, panel_row(x + 3, zh, c) + UNIT * (j - 5),
                    panel_row(x + 3, 1 - zh, c) + HALF + UNIT * (j - 13),
                ),
            )
            device = at_x(1)
        ref = rows(start, UNIT)
        return remote(ref, ref, xs_s.at[way, j], xr_s.at[way, j], device)

    def order(way, g):
        if isinstance(g, int):
            return ((0, 1, 3, 2), (0, 3, 1, 2))[way][g]
        if way == 0:
            return jnp.where(g == 2, 3, jnp.where(g == 3, 2, g))
        return jnp.where(g == 1, 3, jnp.where(g == 2, 1, jnp.where(g == 3, 2, 0)))

    is_source = [zl == 3, zl == 0]

    def z_copy(way, k):
        half = jnp.where(is_source[way], zh, 1 - zh)
        start = panel_row(x + order(way, k // 5), half, c) + UNIT * (k % 5) + HALF * way
        ref = rows(start, UNIT)
        return remote(
            ref, ref, zs_s.at[way, k], zr_s.at[way, k], at_z(1) if way == 0 else at_z(-1)
        )

    def sib_copy(index, start, size):
        ref = rows(start, size)
        return remote(ref, ref, ds_s.at[index], dr_s.at[index], sibling)

    def sib_x(way, t):
        if way == 0:
            start = jnp.where(t == 2, panel_row(x + 2, zh, c), panel_row(x + 1, zh, c) + HALF * (t % 2))
        else:
            start = jnp.where(
                t == 2, panel_row(x + 2, zh, c) + HALF, panel_row(x + 3, zh, c) + HALF * ((t + 1) % 2)
            )
        return sib_copy(2 * t + way, start, HALF)

    def sib_z(way, g):
        start = panel_row(x + order(way, g), 1 - zh, c) + HALF * way
        return sib_copy(6 + 2 * g + way, start, HALF)

    def sib_own():
        ref = rows(own, PANEL)
        return remote(ref, ref, ds_s.at[14], dr_s.at[14], sibling)

    @pl.loop(0, 10)
    def _(j):
        x_copy(0, j).start()
        x_copy(1, j).start()

    for way in (0, 1):
        @pl.when(is_source[way])
        def _():
            @pl.loop(0, 5)
            def _(k):
                z_copy(way, k).start()
    sib_own().start()

    nstate = bt_s.shape[0]
    nhead, length = run_s.shape
    first = lax.broadcasted_iota(jnp.int32, (length, length), 0)
    second = lax.broadcasted_iota(jnp.int32, (length, length), 1)

    def readouts():
        loads[0].wait()
        loads[1].wait()
        bc_t = mm(tok_ref[...], wbc_ref[...]).T
        bt_s[...] = bc_t[:nstate].astype(BF16)
        ct_s[...] = bc_t[nstate:].astype(BF16)
        b_s[...] = bc_t[:nstate].T.astype(BF16)
        c_s[...] = bc_t[nstate:].T.astype(BF16)

    def rates():
        shifted = mm(wdt_ref[...], tok_ref[...], NT)[:nhead] + par_ref[0]
        step = jnp.maximum(shifted, 0.0) + jnp.log1p(jnp.exp(-jnp.abs(shifted)))
        step_s[...] = step
        sig_s[...] = 1.0 / (1.0 + jnp.exp(-shifted))
        upper = jnp.where(first <= second, 1.0, 0.0)
        run = lax.dot_general(
            -par_ref[1] * step, upper, NN, precision=HI, preferred_element_type=F32
        )
        run_s[...] = run
        er_s[...] = jnp.exp(run)
        last = run[:, length - 1 :]
        left_s[...] = jnp.exp(last - run)
        tail_s[...] = left_s[...] * step
        a_own[...] = jnp.broadcast_to(jnp.exp(last), a_own.shape)
        for k in (1, 2, 3):
            a_y(k).start()
        ay[y] = a_own[...]
        st_s[...] = mm(b_s[...], ct_s[...])
        loads[2].wait()

    def two(ref, q):
        return jnp.concatenate(
            [jnp.broadcast_to(ref[pl.ds(2 * q + i, 1), :], (HEAD, length)) for i in (0, 1)], axis=0
        )

    def pair_rows(q):
        return pl.ds(pl.multiple_of(q * PAIR, PAIR), PAIR)

    def a_y(k):
        return remote(a_own, ay.at[y], as_s.at[k - 1], ar_s.at[k - 1], at_y(k))

    def a_z(k):
        return remote(az.at[zl], az.at[zl], as_s.at[k + 2], ar_s.at[k + 2], at_zl(k))

    def head_rows(h):
        return pl.ds(pl.multiple_of(h * HEAD, HEAD), HEAD)

    def group_base(way, g):
        return ((x + order(0, g)) % 4 if way == 0 else g) * group

    src_of = (s_loc, g_loc)
    first_of = (first_f, first_b)
    total_of = (total_f, total_b)
    enter_of = (enter_f, enter_b)
    pass_of = (pass_f, pass_b)
    out_of = (out_f, out_b)
    res_of = (ent, later)
    ys_of = ((0, 1, 2, 3), (3, 2, 1, 0))
    starts = (zl == 0, zl == 3)
    ends = (zl == 3, zl == 0)

    def slice_at(way, g, k):
        start = group_base(way, g) + ((y + k) % 4) * slice_rows
        return pl.ds(pl.multiple_of(start, UNIT), slice_rows)

    def e_first(way, g, k):
        return remote(
            src_of[way].at[slice_at(way, g, k)], first_of[way].at[g, y],
            es_s.at[way, g, k - 1], er_sem.at[way, g, k - 1], at_y(k),
        )

    def e_pass(way, g):
        return remote(
            pass_of[way].at[g], enter_of[way].at[g], es_s.at[way, g, 3], er_sem.at[way, g, 3],
            at_z(1) if way == 0 else at_z(-1),
        )

    def e_push(g, k):
        return remote(
            pass_f.at[g], push_f.at[g, zl], ps_s.at[g, k - 1], pr_s.at[g, k - 1], at_zl(k)
        )

    def e_back(way, g, k):
        return remote(
            out_of[way].at[g, (y + k) % 4], res_of[way].at[slice_at(way, g, 0)],
            es_s.at[way, g, 3 + k], er_sem.at[way, g, 3 + k], at_y(k),
        )

    def begin(way, g):
        for k in (1, 2, 3):
            e_first(way, g, k).start()
        first_of[way][g, y] = src_of[way][slice_at(way, g, 0), :]

    def block_rows(b):
        return pl.ds(pl.multiple_of(b * BLOCK, BLOCK), BLOCK)

    def block_decay(way, g, b):
        h = group_base(way, g) // HEAD + (y * slice_rows + b * BLOCK) // HEAD
        return [ay[s, pl.ds(h, 1), :] for s in range(4)]

    def totals(way, g):
        for k in (1, 2, 3):
            e_first(way, g, k).wait_recv()

        @pl.loop(0, slice_rows // BLOCK)
        def _(b):
            at = block_rows(b)
            d = block_decay(way, g, b)
            ys = ys_of[way]
            t = first_of[way][g, ys[0], at, :].astype(F32)
            for s in ys[1:]:
                t = d[s] * t + first_of[way][g, s, at, :].astype(F32)
            total_of[way][g, at, :] = t
            pass_of[way][g, at, :] = t.astype(BF16)

        if way == 0 and g in PUSHED:
            for k in (1, 2, 3):
                @pl.when(zl + k < 4)
                def _():
                    e_push(g, k).start()
            return

        @pl.when(starts[way])
        def _():
            e_pass(way, g).start()
            enter_of[way][g] = jnp.zeros(enter_of[way].shape[1:], BF16)

    def chain(way, g):
        @pl.when(jnp.logical_not(starts[way]))
        def _():
            e_pass(way, g).wait_recv()

            @pl.when(jnp.logical_not(ends[way]))
            def _():
                @pl.loop(0, slice_rows // BLOCK)
                def _(b):
                    at = block_rows(b)
                    d = block_decay(way, g, b)
                    e = enter_of[way][g, at, :].astype(F32)
                    e = d[0] * d[1] * d[2] * d[3] * e + total_of[way][g, at, :]
                    pass_of[way][g, at, :] = e.astype(BF16)

                e_pass(way, g).start()

        spread(way, g)

    def collect(g):
        for k in (1, 2, 3):
            @pl.when(zl - k >= 0)
            def _():
                e_push(g, k).wait_recv()

        @pl.loop(0, slice_rows // BLOCK)
        def _(b):
            at = block_rows(b)
            h = group_base(0, g) // HEAD + (y * slice_rows + b * BLOCK) // HEAD
            total_f[g, at, :] = jnp.zeros((BLOCK, nstate), F32)
            for s in range(3):
                @pl.when(s < zl)
                def _():
                    e = az[s, pl.ds(h, 1), :] * total_f[g, at, :]
                    total_f[g, at, :] = e + push_f[g, s, at, :].astype(F32)
            enter_f[g, at, :] = total_f[g, at, :].astype(BF16)

        spread(0, g)

    def spread(way, g):
        @pl.loop(0, slice_rows // BLOCK)
        def _(b):
            at = block_rows(b)
            d = block_decay(way, g, b)
            ys = ys_of[way]
            e = enter_of[way][g, at, :].astype(F32)
            for s in ys:
                out_of[way][g, s, at, :] = e.astype(BF16)
                if s != ys[-1]:
                    e = d[s] * e + first_of[way][g, s, at, :].astype(F32)

        for k in (1, 2, 3):
            e_back(way, g, k).start()
        res_of[way][slice_at(way, g, 0), :] = out_of[way][g, y]

    def finish(way, g):
        for k in (1, 2, 3):
            e_back(way, g, k).wait_recv()

    def drain(way, g):
        for k in (1, 2, 3):
            e_first(way, g, k).wait_send()
            e_back(way, g, k).wait_send()

        if way == 0 and g in PUSHED:
            for k in (1, 2, 3):
                @pl.when(zl + k < 4)
                def _():
                    e_push(g, k).wait_send()
            return

        @pl.when(jnp.logical_not(ends[way]))
        def _():
            e_pass(way, g).wait_send()

    side = length // 2
    keep = (
        lax.broadcasted_iota(jnp.int32, (side, side), 0)
        <= lax.broadcasted_iota(jnp.int32, (side, side), 1)
    )
    dst_s[...] = jnp.zeros_like(dst_s)

    def own_states(q):
        at = pair_rows(q)
        g = gy_ref[:, at].astype(F32).T
        gy_t[at, :] = g.astype(BF16)
        scaled = (g * two(er_s, q)).astype(BF16)
        gw[at, :] = scaled
        g_loc[at, :] = mm(scaled, c_s[...]).astype(BF16)

    def mixing(h):
        at = head_rows(h)
        r = run_s[pl.ds(h, 1), :]
        r_col = jnp.broadcast_to(r, (side, length)).T
        e00 = jnp.exp(jnp.where(keep, r[:, :side] - r_col[:side], -1e30))
        e01 = jnp.exp(r[:, side:] - r_col[:side])
        e11 = jnp.exp(jnp.where(keep, r[:, side:] - r_col[side:], -1e30))
        e_all[h, :side, :side] = e00.astype(BF16)
        e_all[h, :side, side:] = e01.astype(BF16)
        e_all[h, side:, side:] = e11.astype(BF16)
        m00 = (e00 * st_s[:side, :side]).astype(BF16)
        m01 = (e01 * st_s[:side, side:]).astype(BF16)
        m11 = (e11 * st_s[side:, side:]).astype(BF16)
        upper = jnp.concatenate([m00, m01], axis=1)
        lower = jnp.concatenate([jnp.zeros_like(m11), m11], axis=1)
        m = jnp.concatenate([upper, lower], axis=0)
        m_all[h] = m
        gx_t[at, :] = mm(gy_t[at, :], m, NT)

    def pull_back(q):
        at = pair_rows(q)
        g = gx_t[at, :] + two(left_s, q) * mm(later[at, :], bt_s[...])
        gx_t[at, :] = g
        g = g * two(step_s, q) + two(par_ref.at[2], q) * gy_t[at, :].astype(F32)
        gx_n[:, at] = g.T.astype(BF16)

    def project(g):
        base = group_base(0, g)
        at = pl.ds(pl.multiple_of(base, group), group)
        x_t[at, :] = mm(wt[at, :], tok_ref[...], NT).astype(BF16)

        for i in range(group_pairs):
            q = base // PAIR + i
            here = pair_rows(q)
            scaled = (x_t[here, :].astype(F32) * two(tail_s, q)).astype(BF16)
            xw[here, :] = scaled
            s_loc[here, :] = mm(scaled, b_s[...]).astype(BF16)

    def inside(h):
        at = head_rows(h)
        xh = x_t[at, :].astype(F32)
        xs = (xh * step_s[pl.ds(h, 1), :]).astype(BF16)
        gy = gy_t[at, :]
        y_t[at, :] = mm(xs, m_all[h])
        pull = mm(xs, gy, TN)
        dst_s[:side, :side] += pull[:side, :side] * e_all[h, :side, :side].astype(F32)
        dst_s[:side, side:] += pull[:side, side:] * e_all[h, :side, side:].astype(F32)
        dst_s[side:, side:] += pull[side:, side:] * e_all[h, side:, side:].astype(F32)

    def outputs(q):
        at = pair_rows(q)
        xq = x_t[at, :].astype(F32)
        inner = y_t[at, :] + two(er_s, q) * mm(ent[at, :], ct_s[...])
        prod = inner * gy_t[at, :].astype(F32)
        back = xq * gx_t[at, :]
        full = inner + two(par_ref.at[2], q) * xq
        y_ref[:, at] = full.T.astype(BF16)
        for i in (0, 1):
            part = slice(i * HEAD, (i + 1) * HEAD)
            acc_a[pl.ds(2 * q + i, 1), :] = jnp.sum(prod[part], axis=0, keepdims=True)
            q_s[pl.ds(2 * q + i, 1), :] = jnp.sum(back[part], axis=0, keepdims=True)
            hr = head_rows(2 * q + i)
            final = a_own[pl.ds(2 * q + i, 1), :] * ent[hr, :].astype(F32) + s_loc[hr, :].astype(F32)
            both = jnp.sum(later[hr, :].astype(F32) * final, axis=0, keepdims=True)
            both_s[pl.ds(2 * q + i, 1), :] = jnp.broadcast_to(
                jnp.sum(both, axis=1, keepdims=True), (1, length)
            )

    wide = dtok_ref.shape[1] // 5

    def columns(n):
        return pl.ds(pl.multiple_of(n * wide, 128), wide)

    def pick(s, table):
        if isinstance(s, int):
            return table.index(s) if s in table else -1
        found = -1
        for i, t in enumerate(table):
            found = jnp.where(s == t, i, found)
        return found

    def when(condition):
        def run(body):
            if not isinstance(condition, bool):
                pl.when(condition)(body)
            elif condition:
                body()

        return run

    def step(s):
        j = s - 2

        @when(0 <= j < XOWN)
        def _():
            for way in (0, 1):
                x_copy(way, j).wait_recv()

            @when(j < 5)
            def _():
                for way in (0, 1):
                    x_copy(way, j + 10).start()

            for way in (0, 1):
                @when(is_source[way] if j + 5 < ZUNITS else False)
                def _():
                    z_copy(way, j + 5).start()

            @when(j % 5 == 4)
            def _():
                for way in (0, 1):
                    sib_x(way, j // 5).start()

        for way in (0, 1):
            away = LAG * (zl if way == 0 else 3 - zl)
            late = s - 4 - away

            @when((late >= 7) & (late < 10))
            def _():
                x_copy(way, late + 8).wait_recv()

            k = s - 2 - away

            @when((k >= 0) & (k < ZUNITS))
            def _():
                z_copy(way, k).wait_recv()

                @when(jnp.logical_not(is_source[way]))
                def _():
                    z_copy(way, k).start()

                @when((k >= 7) & (k < 10))
                def _():
                    x_copy(way, k + 8).start()

                @when((k % 5 == 4) | (k == ZUNITS - 1))
                def _():
                    sib_z(way, k // 5).start()

        @when(s == 5)
        def _():
            for k in (1, 2, 3):
                a_y(k).wait()
            az[zl] = ay[0] * ay[1] * ay[2] * ay[3]
            for k in (1, 2, 3):
                a_z(k).start()

        @when(s == 10)
        def _():
            for k in (1, 2, 3):
                a_z(k).wait()

        b = s - 7

        @when((b >= 0) & (b < 4))
        def _():
            totals(1, b)

        b = s - 8 - 2 * (3 - zl)

        @when((b >= 0) & (b < 4))
        def _():
            chain(1, b)

        g_total = pick(s - 2, ENTER)

        @when(g_total >= 0)
        def _():
            totals(0, g_total)

        @when((s >= ENTER[0] + 3) & (s - 3 - 2 * zl == ENTER[0]) if s < ENTER[0] + 10 else False)
        def _():
            chain(0, 0)

        g_push = pick(s - 4, ENTER)

        @when(g_push in PUSHED)
        def _():
            collect(g_push)

        g_enter = pick(s, ENTER)

        @when(g_enter >= 0)
        def _():
            @when(g_enter == 0)
            def _():
                sib_own().wait_recv()

            @when(g_enter > 0)
            def _():
                sib_copy(4 if g_enter == 3 else g_enter - 1, 0, HALF).wait_recv()
                sib_copy(5 if g_enter == 3 else g_enter + 1, 0, HALF).wait_recv()

            swapped = (0, 2, 1, 3)[g_enter]
            sib_copy(6 + 2 * g_enter, 0, HALF).wait_recv()
            sib_copy(7 + 2 * swapped, 0, HALF).wait_recv()
            project(g_enter)
            begin(0, g_enter)

        @when(s == 0)
        def _():
            readouts()

        @when(s == 2)
        def _():
            rates()

        @when(4 <= s < 8)
        def _():
            for i in range(group_pairs):
                own_states((s - 4) * group_pairs + i)

            begin(1, s - 4)

        @when(8 <= s < 16)
        def _():
            for i in range(nhead // 8):
                mixing((s - 8) * (nhead // 8) + i)

        b = s - 17

        @when((b >= 0) & (b < 4))
        def _():
            finish(1, b)

            for i in range(group_pairs):
                pull_back(b * group_pairs + i)

        def inside_some(first_step, g0, count):
            per = group_heads * count // 5
            n = s - first_step

            @when(0 <= n < 5)
            def _():
                for i in range(per):
                    e = n * per + i
                    g = g0 + e // group_heads
                    inside(group_base(0, g) // HEAD + e % group_heads)

        for some in INSIDE:
            inside_some(*some)

        n = s - DTOK_FROM

        @when(0 <= n < 5)
        def _():
            acc_d[:, columns(n)] = mm(gx_n[...], wt[:, columns(n)])

        g_leave = pick(s, LEAVE)

        @when(g_leave >= 0)
        def _():
            finish(0, g_leave)

            for i in range(group_pairs):
                outputs(group_base(0, g_leave) // PAIR + i)

    for s in range(STEPS):
        step(s)

    dst = dst_s[...].astype(BF16)
    gb_t = mm(ct_s[...], dst, NT) + mm(later[...], xw[...], TN)
    gc_t = mm(bt_s[...], dst) + mm(ent[...], gw[...], TN)
    gbc_s[:, :nstate] = gb_t.T.astype(BF16)
    gbc_s[:, nstate:] = gc_t.T.astype(BF16)
    lower = jnp.where(first >= second, 1.0, 0.0)
    q_all = q_s[...]
    d_log = lax.dot_general(
        acc_a[...] - step_s[...] * q_all, lower, NN, precision=HI, preferred_element_type=F32
    ) + both_s[...]
    g_raw = ((q_all - par_ref[1] * d_log) * sig_s[...]).astype(BF16)

    @pl.loop(0, 5)
    def _(n):
        at = columns(n)
        total = acc_d[:, at] + mm(gbc_s[...], wbc_ref[at, :], NT)
        total = total + mm(g_raw, wdt_ref[:nhead, at], TN)
        dtok_ref[:, at] = total.astype(BF16)

    sib_own().wait_send()
    for t in range(3):
        for way in (0, 1):
            sib_x(way, t).wait_send()
    for g in range(4):
        for way in (0, 1):
            sib_z(way, g).wait_send()

    @pl.loop(0, XUNITS)
    def _(j):
        for way in (0, 1):
            x_copy(way, j).wait_send()

    @pl.loop(0, ZUNITS)
    def _(k):
        for way in (0, 1):
            z_copy(way, k).wait_send()

    for g in range(4):
        for way in (0, 1):
            drain(way, g)


def local(tokens, w_x, w_bc, w_dt, dt_bias, decay_rate, skip_gain, grad_y):
    length, width = tokens.shape[1:]
    hp = grad_y.shape[2]
    heads = dt_bias.shape[0]
    state = w_bc.shape[1] // 2
    piece = hp // 16
    params = jnp.broadcast_to(
        jnp.stack([dt_bias, decay_rate, skip_gain])[:, :, None], (3, heads, length)
    )
    vmem = pl.BlockSpec(memory_space=pltpu.VMEM)
    hbm = pl.BlockSpec(memory_space=pl.ANY)
    flat = pltpu.VMEM((hp, length), BF16)
    wide = pltpu.VMEM((hp, length), F32)
    per_head = pltpu.VMEM((heads, length), F32)
    states = pltpu.VMEM((hp, state), BF16)
    slots = pltpu.VMEM((4, 4, piece, state), BF16)
    single = pltpu.VMEM((4, piece, state), BF16)
    exact = pltpu.VMEM((4, piece, state), F32)
    exchange = [slots, exact, single, single, slots]
    decays = pltpu.VMEM((heads, state), F32)
    dma = pltpu.SemaphoreType.DMA
    y, dtok = pl.pallas_call(
        kernel,
        out_shape=(
            jax.ShapeDtypeStruct((length, hp), BF16),
            jax.ShapeDtypeStruct((length, width), BF16),
        ),
        in_specs=[hbm, hbm, hbm, vmem, vmem, hbm],
        out_specs=(vmem, vmem),
        scratch_shapes=[
            pltpu.VMEM((length, width), BF16), pltpu.VMEM((width, 2 * state), BF16),
            pltpu.VMEM((length, hp), BF16),
            pltpu.VMEM((hp, width), BF16), flat, flat, flat, flat, wide,
            pltpu.VMEM((length, hp), BF16), wide, pltpu.VMEM((length, width), F32),
            pltpu.VMEM((heads, length, length), BF16), pltpu.VMEM((heads, length, length), BF16),
            per_head, per_head, per_head, per_head, per_head, per_head, decays,
            per_head, per_head, per_head,
            pltpu.VMEM((state, length), BF16), pltpu.VMEM((state, length), BF16),
            pltpu.VMEM((length, state), BF16), pltpu.VMEM((length, state), BF16),
            pltpu.VMEM((length, length), F32), pltpu.VMEM((length, length), F32),
            pltpu.VMEM((length, 2 * state), BF16),
            states, states, states, states, *exchange, *exchange,
            pltpu.VMEM((4, heads, state), F32), pltpu.VMEM((4, heads, state), F32), slots,
            dma((4,)), dma((2, XUNITS)), dma((2, XUNITS)), dma((2, ZUNITS)), dma((2, ZUNITS)),
            dma((15,)), dma((15,)), dma((2, 4, 7)), dma((2, 4, 7)), dma((6,)), dma((6,)),
            dma((4, 3)), dma((4, 3)),
        ],
        compiler_params=pltpu.CompilerParams(
            collective_id=0, has_side_effects=True, vmem_limit_bytes=60 << 20
        ),
    )(tokens[0], w_x.T, w_bc, w_dt.T, params, grad_y[0])
    return (y[None], dtok[None])


def solution(mesh):
    placed = (P("dp", "ctx", None), P(None, "dp"), P(), P(), P(), P(), P(), P("dp", "ctx", None))
    return jax.shard_map(
        local,
        mesh=mesh,
        in_specs=placed,
        out_specs=(P("dp", "ctx", None), P("dp", "ctx", None)),
        check_vma=False,
    )
```

```python
import functools

import jax
import jax.numpy as jnp
from jax import lax
from jax.experimental import pallas as pl
from jax.experimental.pallas import tpu as pltpu
from jax.sharding import PartitionSpec as P

MESH = pl.DeviceIdType.MESH
F32 = jnp.float32
BF16 = jnp.bfloat16
HI = lax.Precision.HIGHEST

NN = (((1,), (0,)), ((), ()))
NT = (((1,), (1,)), ((), ()))
TN = (((0,), (0,)), ((), ()))

HEAD = 64
PAIR = 128
PANEL = 160
UNIT = 16
HALF = 80
XUNITS = 18
XOWN = 15
ZUNITS = 17
LAG = 2
AHEAD = 3
STEPS = 33
ENTER = (12, 22, 23, 25)
LEAVE = (24, 28, 30, 32)
INSIDE = ((17, 0, 1), (24, 1, 2), (26, 3, 1))
PUSHED = (1, 2, 3)
BLOCK = 32
DTOK_FROM = 27


def mm(a, b, dims=NN):
    return lax.dot_general(a, b, dims, preferred_element_type=F32)


def kernel(
    tok_in, wt_in, wbc_in, wdt_ref, par_ref, gy_in,
    y_ref, dtok_ref,
    tok_ref, wbc_ref, gy_ref, wt, x_t, gy_t, xw, gw, gx_t, gx_n, y_t, acc_d, e_all, m_all,
    run_s, step_s, sig_s, er_s, tail_s, left_s, a_own, q_s, acc_a, both_s,
    bt_s, ct_s, b_s, c_s, st_s, dst_s, gbc_s,
    s_loc, g_loc, ent, later, first_f, total_f, enter_f, pass_f, out_f,
    first_b, total_b, enter_b, pass_b, out_b, ay,
    az, push_f,
    cp_sem, xs_s, xr_s, zs_s, zr_s, ds_s, dr_s, es_s, er_sem, as_s, ar_s, ps_s, pr_s,
):
    dp = lax.axis_index("dp")
    cx = lax.axis_index("ctx")
    x = dp // 4
    zh = (dp // 2) % 2
    c = dp % 2
    zl = cx // 4
    y = cx % 4
    z = zh * 4 + zl
    group = x_t.shape[0] // 4
    group_heads = group // HEAD
    group_pairs = group // PAIR
    slice_rows = group // 4
    nhead = run_s.shape[0]

    def at_x(k):
        return (((x + k) % 4) * 4 + zh * 2 + c, cx)

    def at_z(k):
        zz = (z + k + 8) % 8
        return (x * 4 + (zz // 4) * 2 + c, (zz % 4) * 4 + y)

    def at_y(k):
        return (dp, zl * 4 + (y + k) % 4)

    def at_zl(k):
        return (dp, ((zl + k + 4) % 4) * 4 + y)

    sibling = (x * 4 + zh * 2 + (1 - c), cx)

    def remote(src, dst, send, recv, device):
        return pltpu.make_async_remote_copy(
            src_ref=src, dst_ref=dst, send_sem=send, recv_sem=recv,
            device_id=device, device_id_type=MESH,
        )

    def panel_row(xx, half, core):
        return ((xx % 4) * 4 + half * 2 + core) * PANEL

    own = pl.multiple_of(panel_row(x, zh, c), UNIT)
    cp = pltpu.make_async_copy(wt_in, wt.at[pl.ds(own, PANEL)], cp_sem.at[0])
    loads = [
        pltpu.make_async_copy(src, dst, cp_sem.at[i + 1])
        for i, (src, dst) in enumerate(((tok_in, tok_ref), (wbc_in, wbc_ref), (gy_in, gy_ref)))
    ]
    cp.start()
    for load in loads:
        load.start()

    barrier = pltpu.get_barrier_semaphore()
    peers = [at_x(1), at_x(3), at_z(1), at_z(-1), sibling]
    peers += [at_y(k) for k in (1, 2, 3)] + [at_zl(k) for k in (1, 2, 3)]
    for peer in peers:
        pl.semaphore_signal(barrier, inc=1, device_id=peer, device_id_type=MESH)
    pl.semaphore_wait(barrier, len(peers))
    cp.wait()

    def rows(start, size):
        return wt.at[pl.ds(pl.multiple_of(start, UNIT), size)]

    def x_copy(way, j):
        if way == 0:
            start = jnp.where(
                j < 10, panel_row(x, zh, c) + UNIT * j,
                jnp.where(
                    j < XOWN, panel_row(x + 1, zh, c) + UNIT * (j - 10),
                    panel_row(x + 1, 1 - zh, c) + UNIT * (j - 13),
                ),
            )
            device = at_x(3)
        else:
            start = jnp.where(
                j < 10, panel_row(x, zh, c) + UNIT * ((j + 5) % 10),
                jnp.where(
                    j < XOWN, panel_row(x + 3, zh, c) + UNIT * (j - 5),
                    panel_row(x + 3, 1 - zh, c) + HALF + UNIT * (j - 13),
                ),
            )
            device = at_x(1)
        ref = rows(start, UNIT)
        return remote(ref, ref, xs_s.at[way, j], xr_s.at[way, j], device)

    def order(way, g):
        if isinstance(g, int):
            return ((0, 1, 3, 2), (0, 3, 1, 2))[way][g]
        if way == 0:
            return jnp.where(g == 2, 3, jnp.where(g == 3, 2, g))
        return jnp.where(g == 1, 3, jnp.where(g == 2, 1, jnp.where(g == 3, 2, 0)))

    is_source = [zl == 3, zl == 0]

    def z_copy(way, k):
        half = jnp.where(is_source[way], zh, 1 - zh)
        start = panel_row(x + order(way, k // 5), half, c) + UNIT * (k % 5) + HALF * way
        ref = rows(start, UNIT)
        return remote(
            ref, ref, zs_s.at[way, k], zr_s.at[way, k], at_z(1) if way == 0 else at_z(-1)
        )

    def sib_copy(index, start, size):
        ref = rows(start, size)
        return remote(ref, ref, ds_s.at[index], dr_s.at[index], sibling)

    def sib_x(way, t):
        if way == 0:
            start = jnp.where(t == 2, panel_row(x + 2, zh, c), panel_row(x + 1, zh, c) + HALF * (t % 2))
        else:
            start = jnp.where(
                t == 2, panel_row(x + 2, zh, c) + HALF, panel_row(x + 3, zh, c) + HALF * ((t + 1) % 2)
            )
        return sib_copy(2 * t + way, start, HALF)

    def sib_z(way, g):
        start = panel_row(x + order(way, g), 1 - zh, c) + HALF * way
        return sib_copy(6 + 2 * g + way, start, HALF)

    def sib_own():
        ref = rows(own, PANEL)
        return remote(ref, ref, ds_s.at[14], dr_s.at[14], sibling)

    @pl.loop(0, AHEAD)
    def _(j):
        x_copy(0, j).start()
        x_copy(1, j).start()

    for way in (0, 1):
        @pl.when(is_source[way])
        def _():
            @pl.loop(0, AHEAD)
            def _(k):
                z_copy(way, k).start()
    sib_own().start()

    nstate = bt_s.shape[0]
    nhead, length = run_s.shape
    first = lax.broadcasted_iota(jnp.int32, (length, length), 0)
    second = lax.broadcasted_iota(jnp.int32, (length, length), 1)

    def readouts():
        loads[0].wait()
        loads[1].wait()
        bc_t = mm(tok_ref[...], wbc_ref[...]).T
        bt_s[...] = bc_t[:nstate].astype(BF16)
        ct_s[...] = bc_t[nstate:].astype(BF16)
        b_s[...] = bc_t[:nstate].T.astype(BF16)
        c_s[...] = bc_t[nstate:].T.astype(BF16)

    def rates():
        shifted = mm(wdt_ref[...], tok_ref[...], NT)[:nhead] + par_ref[0]
        step = jnp.maximum(shifted, 0.0) + jnp.log1p(jnp.exp(-jnp.abs(shifted)))
        step_s[...] = step
        sig_s[...] = 1.0 / (1.0 + jnp.exp(-shifted))
        upper = jnp.where(first <= second, 1.0, 0.0)
        run = lax.dot_general(
            -par_ref[1] * step, upper, NN, precision=HI, preferred_element_type=F32
        )
        run_s[...] = run
        er_s[...] = jnp.exp(run)
        last = run[:, length - 1 :]
        left_s[...] = jnp.exp(last - run)
        tail_s[...] = left_s[...] * step
        a_own[...] = jnp.broadcast_to(jnp.exp(last), a_own.shape)
        for k in (1, 2, 3):
            a_y(k).start()
        ay[y] = a_own[...]
        st_s[...] = mm(b_s[...], ct_s[...])
        loads[2].wait()

    def two(ref, q):
        return jnp.concatenate(
            [jnp.broadcast_to(ref[pl.ds(2 * q + i, 1), :], (HEAD, length)) for i in (0, 1)], axis=0
        )

    def pair_rows(q):
        return pl.ds(pl.multiple_of(q * PAIR, PAIR), PAIR)

    def a_y(k):
        return remote(a_own, ay.at[y], as_s.at[k - 1], ar_s.at[k - 1], at_y(k))

    def a_z(k):
        return remote(az.at[zl], az.at[zl], as_s.at[k + 2], ar_s.at[k + 2], at_zl(k))

    def head_rows(h):
        return pl.ds(pl.multiple_of(h * HEAD, HEAD), HEAD)

    def group_base(way, g):
        return ((x + order(0, g)) % 4 if way == 0 else g) * group

    src_of = (s_loc, g_loc)
    first_of = (first_f, first_b)
    total_of = (total_f, total_b)
    enter_of = (enter_f, enter_b)
    pass_of = (pass_f, pass_b)
    out_of = (out_f, out_b)
    res_of = (ent, later)
    ys_of = ((0, 1, 2, 3), (3, 2, 1, 0))
    starts = (zl == 0, zl == 3)
    ends = (zl == 3, zl == 0)

    def slice_at(way, g, k):
        start = group_base(way, g) + ((y + k) % 4) * slice_rows
        return pl.ds(pl.multiple_of(start, UNIT), slice_rows)

    def e_first(way, g, k):
        return remote(
            src_of[way].at[slice_at(way, g, k)], first_of[way].at[g, y],
            es_s.at[way, g, k - 1], er_sem.at[way, g, k - 1], at_y(k),
        )

    def e_pass(way, g):
        return remote(
            pass_of[way].at[g], enter_of[way].at[g], es_s.at[way, g, 3], er_sem.at[way, g, 3],
            at_z(1) if way == 0 else at_z(-1),
        )

    def e_push(g, k):
        return remote(
            pass_f.at[g], push_f.at[g, zl], ps_s.at[g, k - 1], pr_s.at[g, k - 1], at_zl(k)
        )

    def e_back(way, g, k):
        return remote(
            out_of[way].at[g, (y + k) % 4], res_of[way].at[slice_at(way, g, 0)],
            es_s.at[way, g, 3 + k], er_sem.at[way, g, 3 + k], at_y(k),
        )

    def begin(way, g):
        for k in (1, 2, 3):
            e_first(way, g, k).start()
        first_of[way][g, y] = src_of[way][slice_at(way, g, 0), :]

    def block_rows(b):
        return pl.ds(pl.multiple_of(b * BLOCK, BLOCK), BLOCK)

    def block_decay(way, g, b):
        h = group_base(way, g) // HEAD + (y * slice_rows + b * BLOCK) // HEAD
        return [ay[s, pl.ds(h, 1), :] for s in range(4)]

    def totals(way, g):
        for k in (1, 2, 3):
            e_first(way, g, k).wait_recv()

        @pl.loop(0, slice_rows // BLOCK)
        def _(b):
            at = block_rows(b)
            d = block_decay(way, g, b)
            ys = ys_of[way]
            t = first_of[way][g, ys[0], at, :].astype(F32)
            for s in ys[1:]:
                t = d[s] * t + first_of[way][g, s, at, :].astype(F32)
            total_of[way][g, at, :] = t
            pass_of[way][g, at, :] = t.astype(BF16)

        if way == 0 and g in PUSHED:
            for k in (1, 2, 3):
                @pl.when(zl + k < 4)
                def _():
                    e_push(g, k).start()
            return

        @pl.when(starts[way])
        def _():
            e_pass(way, g).start()
            enter_of[way][g] = jnp.zeros(enter_of[way].shape[1:], BF16)

    def chain(way, g):
        @pl.when(jnp.logical_not(starts[way]))
        def _():
            e_pass(way, g).wait_recv()

            @pl.when(jnp.logical_not(ends[way]))
            def _():
                @pl.loop(0, slice_rows // BLOCK)
                def _(b):
                    at = block_rows(b)
                    d = block_decay(way, g, b)
                    e = enter_of[way][g, at, :].astype(F32)
                    e = d[0] * d[1] * d[2] * d[3] * e + total_of[way][g, at, :]
                    pass_of[way][g, at, :] = e.astype(BF16)

                e_pass(way, g).start()

        spread(way, g)

    def collect(g):
        for k in (1, 2, 3):
            @pl.when(zl - k >= 0)
            def _():
                e_push(g, k).wait_recv()

        @pl.loop(0, slice_rows // BLOCK)
        def _(b):
            at = block_rows(b)
            h = group_base(0, g) // HEAD + (y * slice_rows + b * BLOCK) // HEAD
            total_f[g, at, :] = jnp.zeros((BLOCK, nstate), F32)
            for s in range(3):
                @pl.when(s < zl)
                def _():
                    e = az[s, pl.ds(h, 1), :] * total_f[g, at, :]
                    total_f[g, at, :] = e + push_f[g, s, at, :].astype(F32)
            enter_f[g, at, :] = total_f[g, at, :].astype(BF16)

        spread(0, g)

    def spread(way, g):
        @pl.loop(0, slice_rows // BLOCK)
        def _(b):
            at = block_rows(b)
            d = block_decay(way, g, b)
            ys = ys_of[way]
            e = enter_of[way][g, at, :].astype(F32)
            for s in ys:
                out_of[way][g, s, at, :] = e.astype(BF16)
                if s != ys[-1]:
                    e = d[s] * e + first_of[way][g, s, at, :].astype(F32)

        for k in (1, 2, 3):
            e_back(way, g, k).start()
        res_of[way][slice_at(way, g, 0), :] = out_of[way][g, y]

    def finish(way, g):
        for k in (1, 2, 3):
            e_back(way, g, k).wait_recv()

    def drain(way, g):
        for k in (1, 2, 3):
            e_first(way, g, k).wait_send()
            e_back(way, g, k).wait_send()

        if way == 0 and g in PUSHED:
            for k in (1, 2, 3):
                @pl.when(zl + k < 4)
                def _():
                    e_push(g, k).wait_send()
            return

        @pl.when(jnp.logical_not(ends[way]))
        def _():
            e_pass(way, g).wait_send()

    side = length // 2
    keep = (
        lax.broadcasted_iota(jnp.int32, (side, side), 0)
        <= lax.broadcasted_iota(jnp.int32, (side, side), 1)
    )
    dst_s[...] = jnp.zeros_like(dst_s)

    def own_states(q):
        at = pair_rows(q)
        g = gy_ref[:, at].astype(F32).T
        gy_t[at, :] = g.astype(BF16)
        scaled = (g * two(er_s, q)).astype(BF16)
        gw[at, :] = scaled
        g_loc[at, :] = mm(scaled, c_s[...]).astype(BF16)

    def mixing(h):
        at = head_rows(h)
        r = run_s[pl.ds(h, 1), :]
        r_col = jnp.broadcast_to(r, (side, length)).T
        e00 = jnp.exp(jnp.where(keep, r[:, :side] - r_col[:side], -1e30))
        e01 = jnp.exp(r[:, side:] - r_col[:side])
        e11 = jnp.exp(jnp.where(keep, r[:, side:] - r_col[side:], -1e30))
        e_all[h, :side, :side] = e00.astype(BF16)
        e_all[h, :side, side:] = e01.astype(BF16)
        e_all[h, side:, side:] = e11.astype(BF16)
        m00 = (e00 * st_s[:side, :side]).astype(BF16)
        m01 = (e01 * st_s[:side, side:]).astype(BF16)
        m11 = (e11 * st_s[side:, side:]).astype(BF16)
        upper = jnp.concatenate([m00, m01], axis=1)
        lower = jnp.concatenate([jnp.zeros_like(m11), m11], axis=1)
        m = jnp.concatenate([upper, lower], axis=0)
        m_all[h] = m
        gx_t[at, :] = mm(gy_t[at, :], m, NT)

    def pull_back(q):
        at = pair_rows(q)
        g = gx_t[at, :] + two(left_s, q) * mm(later[at, :], bt_s[...])
        gx_t[at, :] = g
        g = g * two(step_s, q) + two(par_ref.at[2], q) * gy_t[at, :].astype(F32)
        gx_n[:, at] = g.T.astype(BF16)

    def project(g):
        base = group_base(0, g)
        at = pl.ds(pl.multiple_of(base, group), group)
        x_t[at, :] = mm(wt[at, :], tok_ref[...], NT).astype(BF16)

        for i in range(group_pairs):
            q = base // PAIR + i
            here = pair_rows(q)
            scaled = (x_t[here, :].astype(F32) * two(tail_s, q)).astype(BF16)
            xw[here, :] = scaled
            s_loc[here, :] = mm(scaled, b_s[...]).astype(BF16)

    def inside(h):
        at = head_rows(h)
        xh = x_t[at, :].astype(F32)
        xs = (xh * step_s[pl.ds(h, 1), :]).astype(BF16)
        gy = gy_t[at, :]
        y_t[at, :] = mm(xs, m_all[h])
        pull = mm(xs, gy, TN)
        dst_s[:side, :side] += pull[:side, :side] * e_all[h, :side, :side].astype(F32)
        dst_s[:side, side:] += pull[:side, side:] * e_all[h, :side, side:].astype(F32)
        dst_s[side:, side:] += pull[side:, side:] * e_all[h, side:, side:].astype(F32)

    def outputs(q):
        at = pair_rows(q)
        xq = x_t[at, :].astype(F32)
        inner = y_t[at, :] + two(er_s, q) * mm(ent[at, :], ct_s[...])
        prod = inner * gy_t[at, :].astype(F32)
        back = xq * gx_t[at, :]
        full = inner + two(par_ref.at[2], q) * xq
        y_ref[:, at] = full.T.astype(BF16)
        for i in (0, 1):
            part = slice(i * HEAD, (i + 1) * HEAD)
            acc_a[pl.ds(2 * q + i, 1), :] = jnp.sum(prod[part], axis=0, keepdims=True)
            q_s[pl.ds(2 * q + i, 1), :] = jnp.sum(back[part], axis=0, keepdims=True)
            hr = head_rows(2 * q + i)
            final = a_own[pl.ds(2 * q + i, 1), :] * ent[hr, :].astype(F32) + s_loc[hr, :].astype(F32)
            both = jnp.sum(later[hr, :].astype(F32) * final, axis=0, keepdims=True)
            both_s[pl.ds(2 * q + i, 1), :] = jnp.broadcast_to(
                jnp.sum(both, axis=1, keepdims=True), (1, length)
            )

    wide = dtok_ref.shape[1] // 5

    def columns(n):
        return pl.ds(pl.multiple_of(n * wide, 128), wide)

    def pick(s, table):
        if isinstance(s, int):
            return table.index(s) if s in table else -1
        found = -1
        for i, t in enumerate(table):
            found = jnp.where(s == t, i, found)
        return found

    def when(condition):
        def run(body):
            if not isinstance(condition, bool):
                pl.when(condition)(body)
            elif condition:
                body()

        return run

    def step(s):
        j = s - 2

        @when(0 <= j < XOWN)
        def _():
            for way in (0, 1):
                x_copy(way, j).wait_recv()

            @when(j + AHEAD < XOWN)
            def _():
                for way in (0, 1):
                    x_copy(way, j + AHEAD).start()

            for way in (0, 1):
                @when(is_source[way] if j + AHEAD < ZUNITS else False)
                def _():
                    z_copy(way, j + AHEAD).start()

            @when(j % 5 == 4)
            def _():
                for way in (0, 1):
                    sib_x(way, j // 5).start()

        for way in (0, 1):
            away = LAG * (zl if way == 0 else 3 - zl)
            late = s - 4 - away

            @when((late >= 7) & (late < 10))
            def _():
                x_copy(way, late + 8).wait_recv()

            k = s - 2 - away

            @when((k >= 0) & (k < ZUNITS))
            def _():
                z_copy(way, k).wait_recv()

                @when(jnp.logical_not(is_source[way]))
                def _():
                    z_copy(way, k).start()

                @when((k >= 7) & (k < 10))
                def _():
                    x_copy(way, k + 8).start()

                @when((k % 5 == 4) | (k == ZUNITS - 1))
                def _():
                    sib_z(way, k // 5).start()

        @when(s == 5)
        def _():
            for k in (1, 2, 3):
                a_y(k).wait()
            az[zl] = ay[0] * ay[1] * ay[2] * ay[3]
            for k in (1, 2, 3):
                a_z(k).start()

        @when(s == 10)
        def _():
            for k in (1, 2, 3):
                a_z(k).wait()

        b = s - 7

        @when((b >= 0) & (b < 4))
        def _():
            totals(1, b)

        b = s - 8 - 2 * (3 - zl)

        @when((b >= 0) & (b < 4))
        def _():
            chain(1, b)

        g_total = pick(s - 2, ENTER)

        @when(g_total >= 0)
        def _():
            totals(0, g_total)

        @when((s >= ENTER[0] + 3) & (s - 3 - 2 * zl == ENTER[0]) if s < ENTER[0] + 10 else False)
        def _():
            chain(0, 0)

        g_push = pick(s - 4, ENTER)

        @when(g_push in PUSHED)
        def _():
            collect(g_push)

        g_enter = pick(s, ENTER)

        @when(g_enter >= 0)
        def _():
            @when(g_enter == 0)
            def _():
                sib_own().wait_recv()

            @when(g_enter > 0)
            def _():
                sib_copy(4 if g_enter == 3 else g_enter - 1, 0, HALF).wait_recv()
                sib_copy(5 if g_enter == 3 else g_enter + 1, 0, HALF).wait_recv()

            swapped = (0, 2, 1, 3)[g_enter]
            sib_copy(6 + 2 * g_enter, 0, HALF).wait_recv()
            sib_copy(7 + 2 * swapped, 0, HALF).wait_recv()
            project(g_enter)
            begin(0, g_enter)

        @when(s == 0)
        def _():
            readouts()

        @when(s == 2)
        def _():
            rates()

        @when(4 <= s < 8)
        def _():
            for i in range(group_pairs):
                own_states((s - 4) * group_pairs + i)

            begin(1, s - 4)

        @when(8 <= s < 16)
        def _():
            for i in range(nhead // 8):
                mixing((s - 8) * (nhead // 8) + i)

        b = s - 17

        @when((b >= 0) & (b < 4))
        def _():
            finish(1, b)

            for i in range(group_pairs):
                pull_back(b * group_pairs + i)

        def inside_some(first_step, g0, count):
            per = group_heads * count // 5
            n = s - first_step

            @when(0 <= n < 5)
            def _():
                for i in range(per):
                    e = n * per + i
                    g = g0 + e // group_heads
                    inside(group_base(0, g) // HEAD + e % group_heads)

        for some in INSIDE:
            inside_some(*some)

        n = s - DTOK_FROM

        @when(0 <= n < 5)
        def _():
            acc_d[:, columns(n)] = mm(gx_n[...], wt[:, columns(n)])

        g_leave = pick(s, LEAVE)

        @when(g_leave >= 0)
        def _():
            finish(0, g_leave)

            for i in range(group_pairs):
                outputs(group_base(0, g_leave) // PAIR + i)

    for s in range(STEPS):
        step(s)

    dst = dst_s[...].astype(BF16)
    gb_t = mm(ct_s[...], dst, NT) + mm(later[...], xw[...], TN)
    gc_t = mm(bt_s[...], dst) + mm(ent[...], gw[...], TN)
    gbc_s[:, :nstate] = gb_t.T.astype(BF16)
    gbc_s[:, nstate:] = gc_t.T.astype(BF16)
    lower = jnp.where(first >= second, 1.0, 0.0)
    q_all = q_s[...]
    d_log = lax.dot_general(
        acc_a[...] - step_s[...] * q_all, lower, NN, precision=HI, preferred_element_type=F32
    ) + both_s[...]
    g_raw = ((q_all - par_ref[1] * d_log) * sig_s[...]).astype(BF16)

    @pl.loop(0, 5)
    def _(n):
        at = columns(n)
        total = acc_d[:, at] + mm(gbc_s[...], wbc_ref[at, :], NT)
        total = total + mm(g_raw, wdt_ref[:nhead, at], TN)
        dtok_ref[:, at] = total.astype(BF16)

    sib_own().wait_send()
    for t in range(3):
        for way in (0, 1):
            sib_x(way, t).wait_send()
    for g in range(4):
        for way in (0, 1):
            sib_z(way, g).wait_send()

    @pl.loop(0, XUNITS)
    def _(j):
        for way in (0, 1):
            x_copy(way, j).wait_send()

    @pl.loop(0, ZUNITS)
    def _(k):
        for way in (0, 1):
            z_copy(way, k).wait_send()

    for g in range(4):
        for way in (0, 1):
            drain(way, g)


def local(tokens, w_x, w_bc, w_dt, dt_bias, decay_rate, skip_gain, grad_y):
    length, width = tokens.shape[1:]
    hp = grad_y.shape[2]
    heads = dt_bias.shape[0]
    state = w_bc.shape[1] // 2
    piece = hp // 16
    params = jnp.broadcast_to(
        jnp.stack([dt_bias, decay_rate, skip_gain])[:, :, None], (3, heads, length)
    )
    vmem = pl.BlockSpec(memory_space=pltpu.VMEM)
    hbm = pl.BlockSpec(memory_space=pl.ANY)
    flat = pltpu.VMEM((hp, length), BF16)
    wide = pltpu.VMEM((hp, length), F32)
    per_head = pltpu.VMEM((heads, length), F32)
    states = pltpu.VMEM((hp, state), BF16)
    slots = pltpu.VMEM((4, 4, piece, state), BF16)
    single = pltpu.VMEM((4, piece, state), BF16)
    exact = pltpu.VMEM((4, piece, state), F32)
    exchange = [slots, exact, single, single, slots]
    decays = pltpu.VMEM((heads, state), F32)
    dma = pltpu.SemaphoreType.DMA
    y, dtok = pl.pallas_call(
        kernel,
        out_shape=(
            jax.ShapeDtypeStruct((length, hp), BF16),
            jax.ShapeDtypeStruct((length, width), BF16),
        ),
        in_specs=[hbm, hbm, hbm, vmem, vmem, hbm],
        out_specs=(vmem, vmem),
        scratch_shapes=[
            pltpu.VMEM((length, width), BF16), pltpu.VMEM((width, 2 * state), BF16),
            pltpu.VMEM((length, hp), BF16),
            pltpu.VMEM((hp, width), BF16), flat, flat, flat, flat, wide,
            pltpu.VMEM((length, hp), BF16), wide, pltpu.VMEM((length, width), F32),
            pltpu.VMEM((heads, length, length), BF16), pltpu.VMEM((heads, length, length), BF16),
            per_head, per_head, per_head, per_head, per_head, per_head, decays,
            per_head, per_head, per_head,
            pltpu.VMEM((state, length), BF16), pltpu.VMEM((state, length), BF16),
            pltpu.VMEM((length, state), BF16), pltpu.VMEM((length, state), BF16),
            pltpu.VMEM((length, length), F32), pltpu.VMEM((length, length), F32),
            pltpu.VMEM((length, 2 * state), BF16),
            states, states, states, states, *exchange, *exchange,
            pltpu.VMEM((4, heads, state), F32), pltpu.VMEM((4, heads, state), F32), slots,
            dma((4,)), dma((2, XUNITS)), dma((2, XUNITS)), dma((2, ZUNITS)), dma((2, ZUNITS)),
            dma((15,)), dma((15,)), dma((2, 4, 7)), dma((2, 4, 7)), dma((6,)), dma((6,)),
            dma((4, 3)), dma((4, 3)),
        ],
        compiler_params=pltpu.CompilerParams(
            collective_id=0, has_side_effects=True, vmem_limit_bytes=60 << 20
        ),
    )(tokens[0], w_x.T, w_bc, w_dt.T, params, grad_y[0])
    return (y[None], dtok[None])


def solution(mesh):
    placed = (P("dp", "ctx", None), P(None, "dp"), P(), P(), P(), P(), P(), P("dp", "ctx", None))
    return jax.shard_map(
        local,
        mesh=mesh,
        in_specs=placed,
        out_specs=(P("dp", "ctx", None), P("dp", "ctx", None)),
        check_vma=False,
    )
```
